128 devices in a mesh: section: 8 (over x, core), space: 16 (over z, y).
Axes of the slice: x: 4, y: 4, z: 4, core: 2. Of those that a mesh axis runs over, the one named last changes fastest.
Arguments:
- volume: bfloat16 [8, 32, 8, 8, 64], P('section', 'space'), may hold values from -6 to 6
- w_first: bfloat16 [1728, 128], replicated, may hold values from -0.25 to 0.25
- w_enc: bfloat16 [3456, 128], replicated, may hold values from -0.1875 to 0.1875
- w_down: bfloat16 [1024, 256], replicated, may hold values from -0.25 to 0.25
- w_bottom: bfloat16 [6912, 256], replicated, may hold values from -0.125 to 0.125
- w_up: bfloat16 [256, 1024], replicated, may hold values from -0.375 to 0.375
- w_join: bfloat16 [6912, 128], replicated, may hold values from -0.125 to 0.125
- cotangent: bfloat16 [8, 32, 8, 8, 128], P('section', 'space'), may hold values from -6 to 6
Outputs:
- decoded: bfloat16 [8, 32, 8, 8, 128], P('section', 'space')
- grad_first: float32 [1728, 128], P(None, 'space')
- grad_enc: float32 [3456, 128], P(None, 'space')
- grad_down: float32 [1024, 256], P(None, 'space')
- grad_bottom: float32 [6912, 256], P(None, 'space')
- grad_up: float32 [256, 1024], P(None, 'space')
- grad_join: float32 [6912, 128], P(None, 'space')
The draws below stay inside these ranges and needn't reach their ends.
All inputs are finite; a program needn't handle non-finite values.
Results may differ from the reference program's by a relative error of at most 0.025.
Values may be sent and summed in bfloat16 or wider, within the bound.
A program may use at most 128 MiB of HBM per device.

```python
import math
import jax
import jax.numpy as jnp
from jax import lax

C0 = 64
C1 = 128
C2 = 256
NY = 8
NZ = 8
CROPS = 8
NX = 32


def shard_levels(rng, shape, shards, low, high):
    loudness, own = 1.0, jax.random.fold_in(rng, 6)
    for position, blocks in shards:
        steps = jnp.exp(jax.random.uniform(jax.random.fold_in(own, position), (blocks,), jnp.float32, low / len(shards), high / len(shards)))
        loudness = loudness * jnp.repeat(steps, shape[position] // blocks).reshape([-1 if axis == position else 1 for axis in range(len(shape))])
    return loudness


def scatter_about(own_key, extent, scale, reach, pieces=(), kind=jnp.bfloat16):
    factor_of = shard_levels(own_key, extent, pieces, -0.22, 0.18) if pieces else 1.0
    values = jax.random.normal(own_key, extent, jnp.float32) * scale * factor_of
    return jnp.minimum(jnp.maximum(values, -reach), reach).astype(kind)


def setup_inputs(seed: int = 0) -> dict:
    key_of = jax.random.split(jax.random.key(seed), 9)
    volume = scatter_about(key_of[0], (CROPS, NX, NY, NZ, C0), 1.0, 6.0, ((0, 8), (1, 16)))
    w_first = scatter_about(key_of[1], (27 * C0, C1), (9 * C0) ** -0.5, 0.25)
    w_enc = scatter_about(key_of[2], (27 * C1, C1), (9 * C1) ** -0.5, 0.1875)
    w_down = scatter_about(key_of[3], (8 * C1, C2), (4 * C1) ** -0.5, 0.25)
    w_bottom = scatter_about(key_of[4], (27 * C2, C2), (9 * C2) ** -0.5, 0.125)
    w_up = scatter_about(key_of[5], (C2, 8 * C1), C2 ** -0.5, 0.375)
    w_join = scatter_about(key_of[6], (54 * C1, C1), (18 * C1) ** -0.5, 0.125)
    cotangent = scatter_about(key_of[7], (CROPS, NX, NY, NZ, C1), 1.0, 6.0, ((0, 8), (1, 16)))
    return {"volume": volume, "w_first": w_first, "w_enc": w_enc, "w_down": w_down, "w_bottom": w_bottom, "w_up": w_up, "w_join": w_join, "cotangent": cotangent}


def conv_full(field, weight):
    width_in = field.shape[-1]
    kernel = weight.reshape(3, 3, 3, width_in, weight.shape[-1])
    return lax.conv_general_dilated(field[None], kernel, (1, 1, 1), 'SAME', dimension_numbers=('NDHWC', 'DHWIO', 'NDHWC'), precision=lax.Precision.HIGHEST)[0]

def down_full(field, weight):
    size_x, size_y, size_z, width = field.shape
    blocks = field.reshape(size_x // 2, 2, size_y // 2, 2, size_z // 2, 2, width).transpose(0, 2, 4, 1, 3, 5, 6)
    blocks = blocks.reshape(size_x // 2, size_y // 2, size_z // 2, 8 * width)
    return jnp.dot(blocks, weight, precision=lax.Precision.HIGHEST)

def up_full(field, weight):
    size_x, size_y, size_z, wide = field.shape
    width = weight.shape[1] // 8
    spread = jnp.dot(field, weight, precision=lax.Precision.HIGHEST)
    spread = spread.reshape(size_x, size_y, size_z, 2, 2, 2, width).transpose(0, 3, 1, 4, 2, 5, 6)
    return spread.reshape(2 * size_x, 2 * size_y, 2 * size_z, width)

def silu_slope(pre):
    logistic = jax.nn.sigmoid(pre)
    return logistic * (1.0 + pre * (1.0 - logistic))

def rounded(value):
    return lax.optimization_barrier(value.astype(jnp.bfloat16)).astype(jnp.float32)

def layer(field, weight, action):
    pre = action(field.astype(jnp.float32), weight)
    return (pre, jax.nn.silu(pre).astype(jnp.bfloat16))

def reference(volume, w_first, w_enc, w_down, w_bottom, w_up, w_join, cotangent):
    weights = [item.astype(jnp.float32) for item in (w_first, w_enc, w_down, w_bottom, w_up, w_join)]
    f_first, f_enc, f_down, f_bottom, f_up, f_join = weights
    totals = [jnp.zeros(item.shape, jnp.float32) for item in weights]
    outputs = []
    for crop in range(CROPS):
        field = volume[crop]
        pre_first, act_first = layer(field, f_first, conv_full)
        pre_enc, skip_map = layer(act_first, f_enc, conv_full)
        pre_down, act_down = layer(skip_map, f_down, down_full)
        pre_bottom, act_bottom = layer(act_down, f_bottom, conv_full)
        lifted = up_full(act_bottom.astype(jnp.float32), f_up).astype(jnp.bfloat16)
        joined = jnp.concatenate([lifted, skip_map], axis=-1)
        pre_join, out_map = layer(joined, f_join, conv_full)
        outputs.append(out_map)
        step_join = rounded(cotangent[crop].astype(jnp.float32) * silu_slope(pre_join))
        unused, pull = jax.vjp(conv_full, joined.astype(jnp.float32), f_join)
        back, grad_w = pull(step_join)
        totals[5] = totals[5] + grad_w
        grad_lift = rounded(back[..., :C1])
        grad_skip = back[..., C1:]
        unused, pull = jax.vjp(up_full, act_bottom.astype(jnp.float32), f_up)
        back, grad_w = pull(grad_lift)
        totals[4] = totals[4] + grad_w
        step_bottom = rounded(rounded(back) * silu_slope(pre_bottom))
        unused, pull = jax.vjp(conv_full, act_down.astype(jnp.float32), f_bottom)
        back, grad_w = pull(step_bottom)
        totals[3] = totals[3] + grad_w
        step_down = rounded(rounded(back) * silu_slope(pre_down))
        unused, pull = jax.vjp(down_full, skip_map.astype(jnp.float32), f_down)
        back, grad_w = pull(step_down)
        totals[2] = totals[2] + grad_w
        step_enc = rounded((back + grad_skip) * silu_slope(pre_enc))
        unused, pull = jax.vjp(conv_full, act_first.astype(jnp.float32), f_enc)
        back, grad_w = pull(step_enc)
        totals[1] = totals[1] + grad_w
        step_first = rounded(rounded(back) * silu_slope(pre_first))
        unused, pull = jax.vjp(conv_full, field.astype(jnp.float32), f_first)
        back, grad_w = pull(step_first)
        totals[0] = totals[0] + grad_w
    factor = 1.0 / math.sqrt(CROPS * NX * NY * NZ)
    decoded = jnp.stack(outputs, 0)
    return (decoded, totals[0] * factor, totals[1] * factor, totals[2] * factor, totals[3] * factor, totals[4] * factor, totals[5] * factor)
```

```python
import math

import jax
import jax.numpy as jnp
from jax import lax
from jax.experimental import pallas as pl
from jax.experimental.pallas import tpu as pltpu
from jax.sharding import PartitionSpec as P

BF = jnp.bfloat16
F32 = jnp.float32
MESH = pl.DeviceIdType.MESH
T = 128
GROUPS = ((0, 32), (32, 64), (96, 24), (120, 8))
JOIN_AT, UP_AT, BOTTOM_AT, DOWN_AT, ENC_AT, FIRST_AT = 0, 32, 40, 96, 104, 120
PADS = ((27, 32), (94, 96), (118, 120), (127, 128))
COLS = 128 * T
HALF, EIGHTH = COLS // 2, COLS // 8


def mm(a, b):
    return jnp.dot(a, b, preferred_element_type=F32)


def mm_t(a, b):
    return lax.dot_general(a, b, (((1,), (1,)), ((), ())), preferred_element_type=F32)


def silu(z):
    return z * jax.nn.sigmoid(z)


def slope(z):
    s = jax.nn.sigmoid(z)
    return s * (1.0 + z * (1.0 - s))


def one_hot(cond):
    return jnp.where(cond, 1.0, 0.0).astype(BF)


def iotas(shape):
    return lax.broadcasted_iota(jnp.int32, shape, 0), lax.broadcasted_iota(jnp.int32, shape, 1)


def block_row(v):
    y, z = (v >> 3) & 7, v & 7
    return ((v >> 6) * 4 + (y & 1) * 2 + (z & 1)) * 16 + (y >> 1) * 4 + (z >> 1)


def ds(at, size):
    return pl.ds(pl.multiple_of(at, T), size)


def kernel(
    vol_h, wf_h, we_h, wd_h, wb_h, wu_h, wj_h, cot_h,
    dec_o, gf_o, ge_o, gd_o, gb_o, gu_o, gj_o,
    vol, wf, we, wd, wb, wu, wj, cot, load_sem,
    shift, shift_c, perm, perm_t, eye, half_mask,
    a_f, a_e, a_j, a_s, a_b, b_b, blocks, diag,
    z1, z2, e_skip,
    h1, sk, li, t7, t2, g1, t4,
    hv, hr, hc, h_send, h_recv,
    packed, r0, u0, r1, u1, r2, u2, r3, u3, full,
    s0, q0, s1, q1, s2, q2, s3, q3, s4, q4,
):
    sec, me = lax.axis_index("section"), lax.axis_index("space")
    core, my_x = sec % 2, sec // 2
    my_z, my_y = me // 4, me % 4

    loads = []
    for i, (src, dst) in enumerate(
        ((vol_h, vol), (wf_h, wf.at[pl.ds(0, 1728)]), (we_h, we), (wd_h, wd), (wb_h, wb), (wu_h, wu), (cot_h, cot), (wj_h, wj))
    ):
        copy = pltpu.make_async_copy(src, dst, load_sem.at[i])
        copy.start()
        loads.append(copy)
    l_vol, l_wf, l_we, l_wd, l_wb, l_wu, l_cot, l_wj = loads

    after, before = (sec, (me + 1) % 16), (sec, (me + 15) % 16)
    other_core = (sec + 1 - 2 * core, me)
    y_peers = [(sec, my_z * 4 + (my_y + d) % 4) for d in (1, 2, 3)]
    z_peers = [(sec, ((my_z + d) % 4) * 4 + my_y) for d in (1, 2, 3)]
    sec_peers = [((sec + d) % 8, me) for d in range(1, 8)]

    barrier = pltpu.get_barrier_semaphore()
    peers = [after, before, *y_peers, *z_peers, *sec_peers]
    for dev in peers:
        pl.semaphore_signal(barrier, inc=1, device_id=dev, device_id_type=MESH)

    r, c = iotas((64, 64))
    for k in range(9):
        oy, oz = k // 3 - 1, k % 3 - 1
        shift[k] = one_hot(((c >> 3) == (r >> 3) + oy) & ((c & 7) == (r & 7) + oz))
    r, c = iotas((16, 16))
    for k in range(9):
        oy, oz = k // 3 - 1, k % 3 - 1
        shift_c[k * 16 : (k + 1) * 16, :] = one_hot(((c >> 2) == (r >> 2) + oy) & ((c & 3) == (r & 3) + oz))
    r, c = iotas((T, T))
    perm[...] = one_hot(r == block_row(c))
    perm_t[...] = one_hot(c == block_row(r))
    half_mask[0] = one_hot(c < 64)
    half_mask[1] = one_hot(c >= 64)
    r, c = iotas((256, 256))
    eye[...] = one_hot(r == c)
    wf[1728:1792, :] = jnp.zeros((64, T), BF)
    a_e[:, 3456:3584] = jnp.zeros((T, T), BF)
    diag[...] = jnp.zeros((T, 2048), BF)
    for lo, hi in PADS:
        packed[:, :, lo * T : hi * T] = jnp.zeros((16, 16, (hi - lo) * T), BF)

    not_first = jnp.where(me > 0, 1.0, 0.0)
    not_last = jnp.where(me < 15, 1.0, 0.0)

    sends = []

    def remote(src, dst, send_sem, recv_sem, dev):
        return pltpu.make_async_remote_copy(
            src_ref=src, dst_ref=dst, send_sem=send_sem, recv_sem=recv_sem, device_id=dev, device_id_type=MESH
        )

    def swap(index, first, last, got):
        up = remote(last, got.at[0], h_send.at[index, 0], h_recv.at[index, 0], after)
        down = remote(first, got.at[1], h_send.at[index, 1], h_recv.at[index, 1], before)
        up.start()
        down.start()
        sends.extend((up, down))
        return up, down

    def swap_fine(index, ref):
        return swap(index, ref.at[pl.ds(0, 64)], ref.at[pl.ds(64, 64)], hr.at[index])

    def arrived(pair, got):
        for copy in pair:
            copy.wait_recv()
        lo = (got[0].astype(F32) * not_first).astype(BF)
        hi = (got[1].astype(F32) * not_last).astype(BF)
        return lo, hi

    def spread(to, pair, places, stride, off):
        both = jnp.concatenate(pair, axis=1)
        for k in range(9):
            moved = mm(shift[k], both).astype(BF)
            for n, spots in enumerate(places):
                for ox, i in spots:
                    at = (ox * 9 + k) * stride + off
                    to[i * 64 : (i + 1) * 64, at : at + T] = moved[:, n * T : (n + 1) * T]

    def spread_own(to, own, stride=T, off=0):
        spread(to, (own[0:64], own[64:128]), (((1, 0), (0, 1)), ((2, 0), (1, 1))), stride, off)

    def spread_halo(to, lo, hi, stride=T, off=0):
        spread(to, (lo, hi), (((0, 0),), ((2, 1),)), stride, off)

    def spread_coarse(to, lo, own, hi):
        moved = mm(shift_c[...], jnp.concatenate([lo, own, hi], axis=1)).astype(BF)
        for ox in range(3):
            for k in range(9):
                at = (ox * 9 + k) * 256
                to[:, at : at + 256] = moved[k * 16 : (k + 1) * 16, ox * 256 : (ox + 1) * 256]

    def stacked(flat):
        return jnp.concatenate([flat[:, t * T : (t + 1) * T] for t in range(8)], axis=0)

    def grad_128(step, a, half_tiles, chunk, tile):
        step_t = mm_t(eye[0:T, 0:T], step).astype(BF)
        width = chunk * T
        for n in range(0, half_tiles, chunk):
            left = mm(step_t, a[:, n * T : n * T + width]).reshape(16, 8, width)
            right = mm(step_t, a[:, (half_tiles + n) * T : (half_tiles + n) * T + width]).reshape(16, 8, width)
            at = (tile + n) * T
            packed[:, :, at : at + width] = jnp.concatenate([left, right], axis=1).astype(BF)

    def grad_256(step, a, tiles, tile):
        step_t = mm_t(eye[...], step).astype(BF)
        for n in range(0, tiles, 2):
            at = (tile + n) * T
            packed[:, :, at : at + 256] = mm(step_t, a[:, n * T : n * T + 256]).reshape(16, 16, 256).astype(BF)

    step_1, step_2 = 1 + 3 * core, 4 - 3 * core
    at_1 = my_y + core * (my_z - my_y)
    at_2 = my_z + core * (my_y - my_z)
    flight = {}

    def peer_1(d):
        return (sec, ((at_1 + d) % 4) * step_1 + at_2 * step_2)

    def peer_2(d):
        return (sec, at_1 * step_1 + ((at_2 + d) % 4) * step_2)

    def stage_0(g):
        first, n = GROUPS[g]
        w = n // 2 * T
        copy = remote(
            packed.at[:, :, ds(first * T + (1 - core) * w, w)],
            r0.at[:, :, pl.ds(first // 2 * T, w)],
            s0.at[g], q0.at[g], other_core,
        )
        copy.start()
        flight[g] = [copy]
        sends.append(copy)

    def stage_1(g):
        first, n = GROUPS[g]
        w, at = n // 2 * T, first // 2 * T
        flight[g][0].wait_recv()
        mine = ds(first * T + core * w, w)

        def add(i, carry):
            for j in range(4):
                p = i * step_1 + j * step_2
                u0[i, j, :, at : at + w] = packed[p, :, mine] + r0[p, :, at : at + w]
            return carry

        lax.fori_loop(0, 4, add, 0)
        flight[g] = []
        for d in (1, 2, 3):
            copy = remote(
                u0.at[(at_1 + d) % 4, :, :, pl.ds(at, w)],
                r1.at[d - 1, :, :, pl.ds(at, w)],
                s1.at[g, d - 1], q1.at[g, d - 1], peer_1(d),
            )
            copy.start()
            flight[g].append(copy)
            sends.append(copy)

    def stage_2(g):
        first, n = GROUPS[g]
        w, at = n // 2 * T, first // 2 * T
        for copy in flight[g]:
            copy.wait_recv()

        def add(j, carry):
            total = u0[at_1, j, :, at : at + w].astype(F32)
            for d in range(3):
                total = total + r1[d, j, :, at : at + w].astype(F32)
            u1[j, :, at : at + w] = total.astype(BF)
            return carry

        lax.fori_loop(0, 4, add, 0)
        flight[g] = []
        for d in (1, 2, 3):
            copy = remote(
                u1.at[(at_2 + d) % 4, :, pl.ds(at, w)],
                r2.at[d - 1, :, pl.ds(at, w)],
                s2.at[g, d - 1], q2.at[g, d - 1], peer_2(d),
            )
            copy.start()
            flight[g].append(copy)
            sends.append(copy)

    def stage_3(g):
        first, n = GROUPS[g]
        w, at = n // 2 * T, first // 2 * T
        q = n // 8 * T
        for copy in flight[g]:
            copy.wait_recv()
        total = u1[at_2, :, at : at + w].astype(F32)
        for d in range(3):
            total = total + r2[d, :, at : at + w].astype(F32)
        u2[:, at : at + w] = total.astype(BF)
        flight[g] = []
        for d in (1, 2, 3):
            copy = remote(
                u2.at[:, ds(at + ((my_x + d) % 4) * q, q)],
                r3.at[d - 1, :, pl.ds(first // 8 * T, q)],
                s3.at[g, d - 1], q3.at[g, d - 1], (((my_x + d) % 4) * 2 + core, me),
            )
            copy.start()
            flight[g].append(copy)
            sends.append(copy)

    def stage_4(g):
        first, n = GROUPS[g]
        at = first // 2 * T
        q, fine_at = n // 8 * T, first // 8 * T
        for copy in flight[g]:
            copy.wait_recv()
        total = u2[:, ds(at + my_x * q, q)].astype(F32)
        for d in range(3):
            total = total + r3[d, :, fine_at : fine_at + q].astype(F32)
        done = total.astype(BF)
        u3[:, fine_at : fine_at + q] = done
        flight[g] = []
        for d in range(1, 8):
            place = first * T + core * (n // 2 * T) + my_x * q
            copy = remote(
                u3.at[:, pl.ds(fine_at, q)], full.at[:, ds(place, q)],
                s4.at[g, d - 1], q4.at[g, d - 1], ((sec + d) % 8, me),
            )
            copy.start()
            sends.append(copy)
            src = (sec + 8 - d) % 8
            place = first * T + (src % 2) * (n // 2 * T) + (src // 2) * q
            flight[g].append(
                remote(
                    u3.at[:, pl.ds(fine_at, q)], full.at[:, ds(place, q)],
                    s4.at[g, d - 1], q4.at[g, d - 1], ((sec + d) % 8, me),
                )
            )
        full[:, ds(first * T + core * (n // 2 * T) + my_x * q, q)] = done

    def stage_5(g):
        for copy in flight[g]:
            copy.wait_recv()

    l_vol.wait()
    pl.semaphore_wait(barrier, len(peers))
    pair = swap(5, vol.at[pl.ds(0, 64)], vol.at[pl.ds(64, 64)], hv)
    r, c = iotas((64, T))
    twice = one_hot(r == (c & 63))
    h1[...] = mm(vol[...], twice).astype(BF)
    spread_own(a_s, h1)
    lo, hi = arrived(pair, hv)
    spread_halo(a_s, mm(lo, twice).astype(BF), mm(hi, twice).astype(BF))
    for j in range(14):
        tile = a_s[:, 2 * j * T : (2 * j + 1) * T] * half_mask[0]
        if j < 13:
            tile = tile + a_s[:, (2 * j + 1) * T : (2 * j + 2) * T] * half_mask[1]
        a_f[:, j * T : (j + 1) * T] = tile
    l_wf.wait()
    pre = mm(a_f[...], wf[...])
    z1[...] = pre
    h1[...] = silu(pre).astype(BF)
    pair = swap_fine(0, h1)
    spread_own(a_e, h1)
    l_we.wait()
    spread_halo(a_e, *arrived(pair, hr.at[0]))
    pre = mm(a_e[:, 0:3456], we[...])
    z2[...] = pre
    sk[...] = silu(pre).astype(BF)
    skip_pair = swap_fine(1, sk)
    moved = mm(perm[...], sk[...]).astype(BF)
    for t in range(8):
        blocks[:, t * T : (t + 1) * T] = moved[t * 16 : (t + 1) * 16]
    l_wd.wait()
    z3 = mm(blocks[...], wd[...])
    g1[...] = silu(z3).astype(BF)
    pair = swap(6, g1, g1, hc.at[0])
    spread_own(a_j, sk, 256, T)
    spread_halo(a_j, *arrived(skip_pair, hr.at[1]), 256, T)
    l_wb.wait()
    lo, hi = arrived(pair, hc.at[0])
    spread_coarse(a_b, lo, g1[...], hi)
    z4 = mm(a_b[...], wb[...])
    g2 = silu(z4).astype(BF)
    l_wu.wait()
    lifted = stacked(mm(g2, wu[...]).astype(BF))
    li[...] = mm(perm_t[...], lifted).astype(BF)
    pair = swap_fine(2, li)
    spread_own(a_j, li, 256, 0)
    l_wj.wait()
    l_cot.wait()
    spread_halo(a_j, *arrived(pair, hr.at[2]), 256, 0)
    pre = mm(a_j[...], wj[...])
    dec_o[...] = silu(pre).astype(BF)

    t7[...] = (cot[...].astype(F32) * slope(pre)).astype(BF)
    pair = swap_fine(3, t7)
    grad_128(t7[...], a_j, 27, 3, JOIN_AT)
    stage_0(0)
    spread_own(a_s, t7)
    spread_halo(a_s, *arrived(pair, hr.at[3]))
    back = jnp.zeros((T, 256), F32)
    for tap in range(27):
        back = back + mm_t(a_s[:, (26 - tap) * T : (27 - tap) * T], wj[tap * 256 : (tap + 1) * 256, :])
    e_skip[...] = back[:, T:256]
    moved = mm(perm[...], back[:, 0:T].astype(BF)).astype(BF)
    lift_blocks = jnp.concatenate([moved[t * 16 : (t + 1) * 16] for t in range(8)], axis=1)
    e3 = mm_t(lift_blocks, wu[...]).astype(BF)
    t4[...] = (e3.astype(F32) * slope(z4)).astype(BF)
    pair = swap(7, t4, t4, hc.at[1])
    stage_1(0)
    for t in range(8):
        diag[t * 16 : (t + 1) * 16, t * 256 : (t + 1) * 256] = g2
    moved_t = mm_t(eye[0:T, 0:T], moved).astype(BF)
    for t in range(8):
        up = mm(moved_t, diag[:, t * 256 : (t + 1) * 256]).astype(BF)
        for b in range(8):
            at = UP_AT * T + (b % 4) * 256
            packed[2 * t + b // 4, :, at : at + 256] = up[b * 16 : (b + 1) * 16]
    grad_256(t4[...], a_b, 54, BOTTOM_AT)
    stage_0(1)
    lo, hi = arrived(pair, hc.at[1])
    spread_coarse(b_b, lo, t4[...], hi)
    back = jnp.zeros((16, 256), F32)
    for tap in range(27):
        back = back + mm_t(b_b[:, (26 - tap) * 256 : (27 - tap) * 256], wb[tap * 256 : (tap + 1) * 256, :])
    e4 = back.astype(BF)
    t3 = (e4.astype(F32) * slope(z3)).astype(BF)
    e5 = stacked(mm_t(t3, wd[...]))
    high = e5.astype(BF)
    low = (e5 - high.astype(F32)).astype(BF)
    e5 = mm(perm_t[...], high) + mm(perm_t[...], low)
    t2[...] = ((e5 + e_skip[...]) * slope(z2[...])).astype(BF)
    pair = swap_fine(4, t2)
    stage_1(1)
    grad_256(t3, blocks, 8, DOWN_AT)
    grad_128(t2[...], a_e, 14, 2, ENC_AT)
    stage_0(2)
    stage_2(0)
    spread_own(a_s, t2)
    spread_halo(a_s, *arrived(pair, hr.at[4]))
    back = jnp.zeros((T, T), F32)
    for tap in range(27):
        back = back + mm_t(a_s[:, (26 - tap) * T : (27 - tap) * T], we[tap * T : (tap + 1) * T, :])
    t1 = (back.astype(BF).astype(F32) * slope(z1[...])).astype(BF)
    stage_1(2)
    grad_128(t1, a_f, 7, 1, FIRST_AT)
    stage_0(3)
    stage_3(0)
    stage_1(3)
    stage_4(0)
    stage_2(1)
    stage_2(2)
    stage_2(3)
    stage_3(1)
    stage_3(2)
    stage_3(3)
    stage_4(1)
    stage_4(2)
    stage_4(3)

    factor = 1.0 / math.sqrt(16384)

    def rows(tile, width):
        return full[:, tile * T : tile * T + width].astype(F32) * factor

    stage_5(0)
    both = rows(JOIN_AT, 3456)
    gj_o[:, 0:3456] = both[0:8]
    gj_o[:, 3456:6912] = both[8:16]
    stage_5(1)
    for b in range(4):
        gu_o[b * 16 : (b + 1) * 16, :] = rows(UP_AT + 2 * b, 256)
    gb_o[...] = rows(BOTTOM_AT, 6912)
    stage_5(2)
    gd_o[...] = rows(DOWN_AT, 1024)
    both = rows(ENC_AT, 1792)
    ge_o[:, 0:1792] = both[0:8]
    ge_o[:, 1792:3456] = both[8:16, 0:1664]
    stage_5(3)
    both = rows(FIRST_AT, 896)
    gf_o[:, 0:896] = both[0:8]
    gf_o[:, 896:1728] = both[8:16, 0:832]
    for copy in sends:
        copy.wait_send()


def scratch():
    v, dma = pltpu.VMEM, pltpu.SemaphoreType.DMA
    return [
        v((128, 64), BF), v((1792, 128), BF), v((3456, 128), BF), v((1024, 256), BF), v((6912, 256), BF),
        v((256, 1024), BF), v((6912, 128), BF), v((128, 128), BF), dma((8,)),
        v((9, 64, 64), BF), v((144, 16), BF), v((T, T), BF), v((T, T), BF), v((256, 256), BF), v((2, T, T), BF),
        v((T, 1792), BF), v((T, 3584), BF), v((T, 6912), BF), v((T, 3456), BF), v((16, 6912), BF), v((16, 6912), BF),
        v((16, 1024), BF), v((T, 2048), BF),
        v((T, T), F32), v((T, T), F32), v((T, T), F32),
        v((T, T), BF), v((T, T), BF), v((T, T), BF), v((T, T), BF), v((T, T), BF), v((16, 256), BF), v((16, 256), BF),
        v((2, 64, 64), BF), v((5, 2, 64, T), BF), v((2, 2, 16, 256), BF), dma((8, 2)), dma((8, 2)),
        v((16, 16, COLS), BF), v((16, 16, HALF), BF), v((4, 4, 16, HALF), BF), v((3, 4, 16, HALF), BF),
        v((4, 16, HALF), BF), v((3, 16, HALF), BF), v((16, HALF), BF), v((3, 16, EIGHTH), BF), v((16, EIGHTH), BF),
        v((16, COLS), BF),
        dma((4,)), dma((4,)), dma((4, 3)), dma((4, 3)), dma((4, 3)), dma((4, 3)), dma((4, 3)), dma((4, 3)),
        dma((4, 7)), dma((4, 7)),
    ]


def body(volume, w_first, w_enc, w_down, w_bottom, w_up, w_join, cotangent):
    out = lambda shape, dtype=F32: jax.ShapeDtypeStruct(shape, dtype)
    results = pl.pallas_call(
        kernel,
        out_shape=(
            out((128, 128), BF), out((8, 1728)), out((8, 3456)), out((16, 1024)), out((16, 6912)), out((64, 256)),
            out((8, 6912)),
        ),
        in_specs=[pl.BlockSpec(memory_space=pl.ANY)] * 8,
        out_specs=[pl.BlockSpec(memory_space=pltpu.VMEM)] * 7,
        scratch_shapes=scratch(),
        compiler_params=pltpu.CompilerParams(
            collective_id=0, has_side_effects=True, vmem_limit_bytes=58 * 1024 * 1024
        ),
        name="step",
    )(
        volume.reshape(128, 64), w_first, w_enc, w_down, w_bottom, w_up, w_join, cotangent.reshape(128, 128)
    )
    decoded, *grads = results
    return (decoded.reshape(1, 2, 8, 8, 128), *(g.T for g in grads))


def solution(mesh):
    crops = P("section", "space", None, None, None)
    return jax.shard_map(
        body,
        mesh=mesh,
        in_specs=(crops, P(), P(), P(), P(), P(), P(), crops),
        out_specs=(crops, *([P(None, "space")] * 6)),
        check_vma=False,
    )
```

```python
import math

import jax
import jax.numpy as jnp
from jax import lax
from jax.experimental import pallas as pl
from jax.experimental.pallas import tpu as pltpu
from jax.sharding import PartitionSpec as P

BF = jnp.bfloat16
F32 = jnp.float32
MESH = pl.DeviceIdType.MESH
T = 128
GROUPS = ((0, 32), (32, 64), (96, 24), (120, 8))
JOIN_AT, UP_AT, BOTTOM_AT, DOWN_AT, ENC_AT, FIRST_AT = 0, 32, 40, 96, 104, 120
PADS = ((27, 32), (94, 96), (118, 120), (127, 128))
COLS = 128 * T
HALF, EIGHTH = COLS // 2, COLS // 8


def mm(a, b):
    return jnp.dot(a, b, preferred_element_type=F32)


def mm_t(a, b):
    return lax.dot_general(a, b, (((1,), (1,)), ((), ())), preferred_element_type=F32)


def silu(z):
    return z * jax.nn.sigmoid(z)


def slope(z):
    s = jax.nn.sigmoid(z)
    return s * (1.0 + z * (1.0 - s))


def one_hot(cond):
    return jnp.where(cond, 1.0, 0.0).astype(BF)


def iotas(shape):
    return lax.broadcasted_iota(jnp.int32, shape, 0), lax.broadcasted_iota(jnp.int32, shape, 1)


def block_row(v):
    y, z = (v >> 3) & 7, v & 7
    return ((v >> 6) * 4 + (y & 1) * 2 + (z & 1)) * 16 + (y >> 1) * 4 + (z >> 1)


def ds(at, size):
    return pl.ds(pl.multiple_of(at, T), size)


def kernel(
    vol_h, wf_h, we_h, wd_h, wb_h, wu_h, wj_h, cot_h,
    dec_o, full_o,
    vol, wf, we, wd, wb, wu, wj, cot, load_sem,
    shift, shift_c, perm, perm_t, eye, half_mask,
    wx, b_v, b_1, b_j, b_s, b_c, b_4, a_f, blocks, diag,
    z1, z2, e_skip,
    h1, sk, li, t7, t2, t4,
    h_vol, h_cot, h_t2, h_t4, h_send, h_recv,
    packed, r0, u0, r1, u1, r2, u2, r3, u3, full,
    s0, q0, s1, q1, s2, q2, s3, q3, s4, q4,
):
    sec, me = lax.axis_index("section"), lax.axis_index("space")
    core, my_x = sec % 2, sec // 2
    my_z, my_y = me // 4, me % 4

    loads = []
    for i, (src, dst) in enumerate(
        ((vol_h, vol), (wf_h, wf), (we_h, we), (wd_h, wd), (wb_h, wb), (wu_h, wu), (cot_h, cot), (wj_h, wj))
    ):
        copy = pltpu.make_async_copy(src, dst, load_sem.at[i])
        copy.start()
        loads.append(copy)
    l_vol, l_wf, l_we, l_wd, l_wb, l_wu, l_cot, l_wj = loads

    around = {d: (sec, (me + 16 + d) % 16) for d in (-3, -2, -1, 1, 2, 3)}
    after, before = around[1], around[-1]
    other_core = (sec + 1 - 2 * core, me)
    y_peers = [(sec, my_z * 4 + (my_y + d) % 4) for d in (1, 2, 3)]
    z_peers = [(sec, ((my_z + d) % 4) * 4 + my_y) for d in (1, 2, 3)]
    sec_peers = [((sec + d) % 8, me) for d in range(1, 8)]

    barrier = pltpu.get_barrier_semaphore()
    peers = [*around.values(), *y_peers, *z_peers, *sec_peers]
    for dev in peers:
        pl.semaphore_signal(barrier, inc=1, device_id=dev, device_id_type=MESH)

    r, c = iotas((64, 64))
    for k in range(9):
        oy, oz = k // 3 - 1, k % 3 - 1
        shift[k] = one_hot(((c >> 3) == (r >> 3) + oy) & ((c & 7) == (r & 7) + oz))
    r, c = iotas((16, 16))
    for k in range(9):
        oy, oz = k // 3 - 1, k % 3 - 1
        shift_c[k * 16 : (k + 1) * 16, :] = one_hot(((c >> 2) == (r >> 2) + oy) & ((c & 3) == (r & 3) + oz))
    r, c = iotas((T, T))
    perm[...] = one_hot(r == block_row(c))
    perm_t[...] = one_hot(c == block_row(r))
    half_mask[0] = one_hot(c < 64)
    half_mask[1] = one_hot(c >= 64)
    r, c = iotas((256, 256))
    eye[...] = one_hot(r == c)
    diag[...] = jnp.zeros((T, 2048), BF)
    for lo, hi in PADS:
        packed[:, :, lo * T : hi * T] = jnp.zeros((16, 16, (hi - lo) * T), BF)

    not_first = jnp.where(me > 0, 1.0, 0.0)
    not_last = jnp.where(me < 15, 1.0, 0.0)

    sends = []

    def remote(src, dst, send_sem, recv_sem, dev):
        return pltpu.make_async_remote_copy(
            src_ref=src, dst_ref=dst, send_sem=send_sem, recv_sem=recv_sem, device_id=dev, device_id_type=MESH
        )

    def push(index, src, dst, dev):
        copy = remote(src, dst, h_send.at[index], h_recv.at[index], dev)
        copy.start()
        sends.append(copy)
        return copy

    def swap(index, first, last, got):
        return push(index, last, got.at[0], after), push(index + 1, first, got.at[1], before)

    def arrived(pair, got):
        for copy in pair:
            copy.wait_recv()
        lo = (got[0].astype(F32) * not_first).astype(BF)
        hi = (got[1].astype(F32) * not_last).astype(BF)
        return lo, hi

    def inside(x, first, count, layer_rows):
        layer = lax.broadcasted_iota(jnp.int32, x.shape, 0) // layer_rows + first
        return jnp.where((layer >= 0) & (layer < count), x, 0.0).astype(BF)

    def spread(to, layers, row=0, per=2, width=T):
        step = per * 64 // 64
        for n in range(0, len(layers), step):
            group = layers[n : n + step]
            both = jnp.concatenate(group, axis=1)
            for k in range(9):
                moved = mm(shift[k], both).astype(BF)
                for m in range(len(group)):
                    to[row + (n + m) * 64 : row + (n + m + 1) * 64, k * width : (k + 1) * width] = (
                        moved[:, m * width : (m + 1) * width]
                    )

    def layers_of(x):
        return [x[i : i + 64] for i in range(0, x.shape[0], 64)]

    def spread_coarse(to, layers):
        moved = mm(shift_c[...], jnp.concatenate(layers, axis=1)).astype(BF)
        for n in range(len(layers)):
            for k in range(9):
                to[n * 16 : (n + 1) * 16, k * 256 : (k + 1) * 256] = (
                    moved[k * 16 : (k + 1) * 16, n * 256 : (n + 1) * 256]
                )

    def conv(b, w, count, rows):
        depth = b.shape[1]
        total = mm(b[0:count], w[0:depth, :])
        for ox in (1, 2):
            total = total + mm(b[ox * rows : ox * rows + count], w[ox * depth : (ox + 1) * depth, :])
        return total

    def conv_back(b, w, count, rows):
        cols = b.shape[1] // 9
        depth = w.shape[0] // 27
        total = jnp.zeros((count, depth), F32)
        for ox in range(3):
            for k in range(9):
                tap = ox * 9 + k
                total = total + mm_t(
                    b[(2 - ox) * rows : (2 - ox) * rows + count, (8 - k) * cols : (9 - k) * cols],
                    w[tap * depth : (tap + 1) * depth, :],
                )
        return total

    def stacked(flat):
        return jnp.concatenate([flat[:, t * T : (t + 1) * T] for t in range(8)], axis=0)

    def grad_128(step_t, part, tiles, half, chunk, tile):
        width = chunk * T

        def piece(n):
            if n >= tiles:
                return jnp.zeros((16, 8, width), F32)
            return mm(step_t, part(n)).reshape(16, 8, width)

        for n in range(0, half, chunk):
            at = (tile + n) * T
            packed[:, :, at : at + width] = jnp.concatenate([piece(n), piece(half + n)], axis=1).astype(BF)

    def grad_256(step_t, part, tiles, tile):
        for n in range(0, tiles, 2):
            at = (tile + n) * T
            packed[:, :, at : at + 256] = mm(step_t, part(n)).reshape(16, 16, 256).astype(BF)

    def turned(x):
        return mm_t(eye[0 : x.shape[1], 0 : x.shape[1]], x).astype(BF)

    def window(b, at, rows, count, chunk):
        per = b.shape[1] // T

        def part(n):
            ox, k = n // per, n % per
            begin = at + ox * rows
            return b[begin : begin + count, k * T : (k + chunk) * T]

        return part

    step_1, step_2 = 1 + 3 * core, 4 - 3 * core
    at_1 = my_y + core * (my_z - my_y)
    at_2 = my_z + core * (my_y - my_z)
    flight = {}

    def peer_1(d):
        return (sec, ((at_1 + d) % 4) * step_1 + at_2 * step_2)

    def peer_2(d):
        return (sec, at_1 * step_1 + ((at_2 + d) % 4) * step_2)

    def stage_0(g):
        first, n = GROUPS[g]
        w = n // 2 * T
        copy = remote(
            packed.at[:, :, ds(first * T + (1 - core) * w, w)],
            r0.at[:, :, pl.ds(first // 2 * T, w)],
            s0.at[g], q0.at[g], other_core,
        )
        copy.start()
        flight[g] = [copy]
        sends.append(copy)

    def stage_1(g):
        first, n = GROUPS[g]
        w, at = n // 2 * T, first // 2 * T
        flight[g][0].wait_recv()
        mine = ds(first * T + core * w, w)

        def add(i, carry):
            for j in range(4):
                p = i * step_1 + j * step_2
                u0[i, j, :, at : at + w] = packed[p, :, mine] + r0[p, :, at : at + w]
            return carry

        lax.fori_loop(0, 4, add, 0)
        flight[g] = []
        for d in (1, 2, 3):
            copy = remote(
                u0.at[(at_1 + d) % 4, :, :, pl.ds(at, w)],
                r1.at[d - 1, :, :, pl.ds(at, w)],
                s1.at[g, d - 1], q1.at[g, d - 1], peer_1(d),
            )
            copy.start()
            flight[g].append(copy)
            sends.append(copy)

    def stage_2(g):
        first, n = GROUPS[g]
        w, at = n // 2 * T, first // 2 * T
        for copy in flight[g]:
            copy.wait_recv()

        def add(j, carry):
            total = u0[at_1, j, :, at : at + w].astype(F32)
            for d in range(3):
                total = total + r1[d, j, :, at : at + w].astype(F32)
            u1[j, :, at : at + w] = total.astype(BF)
            return carry

        lax.fori_loop(0, 4, add, 0)
        flight[g] = []
        for d in (1, 2, 3):
            copy = remote(
                u1.at[(at_2 + d) % 4, :, pl.ds(at, w)],
                r2.at[d - 1, :, pl.ds(at, w)],
                s2.at[g, d - 1], q2.at[g, d - 1], peer_2(d),
            )
            copy.start()
            flight[g].append(copy)
            sends.append(copy)

    def stage_3(g):
        first, n = GROUPS[g]
        w, at = n // 2 * T, first // 2 * T
        q = n // 8 * T
        for copy in flight[g]:
            copy.wait_recv()
        total = u1[at_2, :, at : at + w].astype(F32)
        for d in range(3):
            total = total + r2[d, :, at : at + w].astype(F32)
        u2[:, at : at + w] = total.astype(BF)
        flight[g] = []
        for d in (1, 2, 3):
            copy = remote(
                u2.at[:, ds(at + ((my_x + d) % 4) * q, q)],
                r3.at[d - 1, :, pl.ds(first // 8 * T, q)],
                s3.at[g, d - 1], q3.at[g, d - 1], (((my_x + d) % 4) * 2 + core, me),
            )
            copy.start()
            flight[g].append(copy)
            sends.append(copy)

    def stage_4(g):
        first, n = GROUPS[g]
        at = first // 2 * T
        q, fine_at = n // 8 * T, first // 8 * T
        for copy in flight[g]:
            copy.wait_recv()
        total = u2[:, ds(at + my_x * q, q)].astype(F32)
        for d in range(3):
            total = total + r3[d, :, fine_at : fine_at + q].astype(F32)
        done = total.astype(BF)
        u3[:, fine_at : fine_at + q] = done
        flight[g] = []
        for d in range(1, 8):
            place = first * T + core * (n // 2 * T) + my_x * q
            copy = remote(
                u3.at[:, pl.ds(fine_at, q)], full.at[:, ds(place, q)],
                s4.at[g, d - 1], q4.at[g, d - 1], ((sec + d) % 8, me),
            )
            copy.start()
            sends.append(copy)
            src = (sec + 8 - d) % 8
            place = first * T + (src % 2) * (n // 2 * T) + (src // 2) * q
            flight[g].append(
                remote(
                    u3.at[:, pl.ds(fine_at, q)], full.at[:, ds(place, q)],
                    s4.at[g, d - 1], q4.at[g, d - 1], ((sec + d) % 8, me),
                )
            )
        full[:, ds(first * T + core * (n // 2 * T) + my_x * q, q)] = done

    def stage_5(g):
        for copy in flight[g]:
            copy.wait_recv()

    l_vol.wait()
    l_cot.wait()
    pl.semaphore_wait(barrier, len(peers))
    pushed = {}
    for n, d in enumerate((1, -1, 2, -2, 3, -3)):
        pushed[-d] = push(n, vol, h_vol.at[3 - d], around[d])
    cot_pair = swap(6, cot.at[pl.ds(0, 64)], cot.at[pl.ds(64, 64)], h_cot)
    r, c = iotas((64, T))
    twice = one_hot(r == (c & 63))
    l_wf.wait()
    zero = jnp.zeros((64, T), BF)
    for tap in range(27):
        wx[tap * T : tap * T + 64, :] = wf[tap * 64 : (tap + 1) * 64, :]
        wx[tap * T + 64 : (tap + 1) * T, :] = zero
    spread(b_v, layers_of(mm(vol[...], twice).astype(BF)), 6 * 64)
    for d in (-1, 1, -2, 2, -3, 3):
        pushed[d].wait_recv()
        got = inside(mm(h_vol[3 + d], twice), 2 * (me + d), 32, 64)
        spread(b_v, layers_of(got), (3 + d) * T)
    z1_all = conv(b_v, wx, 768, 64)
    z1[...] = z1_all[320:448]
    h1[...] = inside(silu(z1_all), 2 * me - 5, 32, 64)
    spread(b_1, layers_of(h1))
    l_we.wait()
    z2_all = conv(b_1, we, 640, 64)
    z2[...] = z2_all[256:384]
    sk[...] = inside(silu(z2_all), 2 * me - 4, 32, 64)
    for n in range(5):
        moved = mm(perm[...], sk[n * T : (n + 1) * T]).astype(BF)
        for t in range(8):
            blocks[n * 16 : (n + 1) * 16, t * T : (t + 1) * T] = moved[t * 16 : (t + 1) * 16]
    l_wd.wait()
    z3 = mm(blocks[...], wd[...])
    g1 = silu(z3).astype(BF)
    spread_coarse(b_c, [g1[n * 16 : (n + 1) * 16] for n in range(5)])
    l_wb.wait()
    z4 = conv(b_c, wb, 48, 16)
    g2 = inside(silu(z4), me - 1, 16, 16)
    l_wu.wait()
    lifted = mm(g2, wu[...]).astype(BF)
    for n in range(3):
        li[n * T : (n + 1) * T] = mm(perm_t[...], stacked(lifted[n * 16 : (n + 1) * 16])).astype(BF)
    layers = [
        jnp.concatenate([li[n * 64 : (n + 1) * 64], sk[(n + 2) * 64 : (n + 3) * 64]], axis=1) for n in range(6)
    ]
    spread(b_j, layers, 0, 1, 256)
    l_wj.wait()
    z7 = conv(b_j, wj, 256, 64)
    dec_o[...] = silu(z7[64:192]).astype(BF)

    lo, hi = arrived(cot_pair, h_cot)
    cots = jnp.concatenate([lo, cot[...], hi], axis=0)
    t7[...] = (cots.astype(F32) * slope(z7)).astype(BF)
    grad_128(turned(t7[64:192]), window(b_j, 64, 64, T, 3), 54, 27, 3, JOIN_AT)
    stage_0(0)
    spread(b_s, layers_of(t7))
    back = conv_back(b_s, wj, T, 64)
    e_skip[...] = back[:, T:256]
    moved = mm(perm[...], back[:, 0:T].astype(BF)).astype(BF)
    lift_blocks = jnp.concatenate([moved[t * 16 : (t + 1) * 16] for t in range(8)], axis=1)
    e3 = mm_t(lift_blocks, wu[...]).astype(BF)
    t4[...] = (e3.astype(F32) * slope(z4[16:32])).astype(BF)
    pair = swap(8, t4, t4, h_t4)
    stage_1(0)
    for t in range(8):
        diag[t * 16 : (t + 1) * 16, t * 256 : (t + 1) * 256] = g2[16:32]
    moved_t = turned(moved)
    for t in range(8):
        up = mm(moved_t, diag[:, t * 256 : (t + 1) * 256]).astype(BF)
        for b in range(8):
            at = UP_AT * T + (b % 4) * 256
            packed[2 * t + b // 4, :, at : at + 256] = up[b * 16 : (b + 1) * 16]
    grad_256(turned(t4[...]), window(b_c, 16, 16, 16, 2), 54, BOTTOM_AT)
    stage_0(1)
    lo, hi = arrived(pair, h_t4)
    spread_coarse(b_4, [lo, t4[...], hi])
    e4 = conv_back(b_4, wb, 16, 16).astype(BF)
    t3 = (e4.astype(F32) * slope(z3[32:48])).astype(BF)
    e5 = stacked(mm_t(t3, wd[...]))
    high = e5.astype(BF)
    low = (e5 - high.astype(F32)).astype(BF)
    e5 = mm(perm_t[...], high) + mm(perm_t[...], low)
    t2[...] = ((e5 + e_skip[...]) * slope(z2[...])).astype(BF)
    pair = swap(10, t2.at[pl.ds(0, 64)], t2.at[pl.ds(64, 64)], h_t2)
    stage_1(1)
    grad_256(turned(t3), lambda n: blocks[32:48, n * T : (n + 2) * T], 8, DOWN_AT)
    grad_128(turned(t2[...]), window(b_1, 256, 64, T, 1), 27, 14, 1, ENC_AT)
    stage_0(2)
    stage_2(0)
    spread(b_s, layers_of(t2), 64)
    lo, hi = arrived(pair, h_t2)
    spread(b_s, [lo], 0)
    spread(b_s, [hi], 192)
    back = conv_back(b_s, we, T, 64)
    t1 = (back.astype(BF).astype(F32) * slope(z1[...])).astype(BF)
    stage_1(2)
    for j in range(14):
        left, right = (b_v[320 + t // 9 * 64 : 448 + t // 9 * 64, t % 9 * T : (t % 9 + 1) * T] for t in (2 * j, min(2 * j + 1, 26)))
        tile = left * half_mask[0]
        if j < 13:
            tile = tile + right * half_mask[1]
        a_f[:, j * T : (j + 1) * T] = tile
    grad_128(turned(t1), lambda n: a_f[:, n * T : (n + 1) * T], 14, 7, 1, FIRST_AT)
    stage_0(3)
    stage_3(0)
    stage_1(3)
    stage_4(0)
    stage_2(1)
    stage_2(2)
    stage_2(3)
    stage_3(1)
    stage_3(2)
    stage_3(3)
    stage_4(1)
    stage_4(2)
    stage_4(3)
    for g, (first, n) in enumerate(GROUPS):
        stage_5(g)
        full_o[:, first * T : (first + n) * T] = full[:, first * T : (first + n) * T]
    for copy in sends:
        copy.wait_send()


def finish(dec, full, dec_o, gf_o, ge_o, gd_o, gb_o, gu_o, gj_o):
    factor = 1.0 / math.sqrt(16384)
    dec_o[...] = dec[...]

    def rows(tile, width):
        return full[:, tile * T : tile * T + width].astype(F32) * factor

    both = rows(JOIN_AT, 3456)
    gj_o[:, 0:3456] = both[0:8]
    gj_o[:, 3456:6912] = both[8:16]
    for b in range(4):
        gu_o[b * 16 : (b + 1) * 16, :] = rows(UP_AT + 2 * b, 256)
    gb_o[...] = rows(BOTTOM_AT, 6912)
    gd_o[...] = rows(DOWN_AT, 1024)
    both = rows(ENC_AT, 1792)
    ge_o[:, 0:1792] = both[0:8]
    ge_o[:, 1792:3456] = both[8:16, 0:1664]
    both = rows(FIRST_AT, 896)
    gf_o[:, 0:896] = both[0:8]
    gf_o[:, 896:1728] = both[8:16, 0:832]


def scratch():
    v, dma = pltpu.VMEM, pltpu.SemaphoreType.DMA
    return [
        v((128, 64), BF), v((1728, 128), BF), v((3456, 128), BF), v((1024, 256), BF), v((6912, 256), BF),
        v((256, 1024), BF), v((6912, 128), BF), v((128, 128), BF), dma((8,)),
        v((9, 64, 64), BF), v((144, 16), BF), v((T, T), BF), v((T, T), BF), v((256, 256), BF), v((2, T, T), BF),
        v((3456, T), BF), v((896, 1152), BF), v((768, 1152), BF), v((384, 2304), BF), v((256, 1152), BF),
        v((80, 2304), BF), v((48, 2304), BF), v((T, 1792), BF), v((80, 1024), BF), v((T, 2048), BF),
        v((T, T), F32), v((T, T), F32), v((T, T), F32),
        v((768, T), BF), v((640, T), BF), v((384, T), BF), v((256, T), BF), v((T, T), BF), v((16, 256), BF),
        v((7, T, 64), BF), v((2, 64, T), BF), v((2, 64, T), BF), v((2, 16, 256), BF), dma((12,)), dma((12,)),
        v((16, 16, COLS), BF), v((16, 16, HALF), BF), v((4, 4, 16, HALF), BF), v((3, 4, 16, HALF), BF),
        v((4, 16, HALF), BF), v((3, 16, HALF), BF), v((16, HALF), BF), v((3, 16, EIGHTH), BF), v((16, EIGHTH), BF),
        v((16, COLS), BF),
        dma((4,)), dma((4,)), dma((4, 3)), dma((4, 3)), dma((4, 3)), dma((4, 3)), dma((4, 3)), dma((4, 3)),
        dma((4, 7)), dma((4, 7)),
    ]


def body(volume, w_first, w_enc, w_down, w_bottom, w_up, w_join, cotangent):
    out = lambda shape, dtype=F32: jax.ShapeDtypeStruct(shape, dtype)
    done = pl.pallas_call(
        kernel,
        out_shape=(out((128, 128), BF), out((16, COLS), BF)),
        in_specs=[pl.BlockSpec(memory_space=pl.ANY)] * 8,
        out_specs=[pl.BlockSpec(memory_space=pltpu.VMEM)] * 2,
        scratch_shapes=scratch(),
        compiler_params=pltpu.CompilerParams(
            collective_id=0, has_side_effects=True, vmem_limit_bytes=58 * 1024 * 1024
        ),
        name="step",
    )(
        volume.reshape(128, 64), w_first, w_enc, w_down, w_bottom, w_up, w_join, cotangent.reshape(128, 128)
    )
    results = pl.pallas_call(
        finish,
        out_shape=(
            out((128, 128), BF), out((8, 1728)), out((8, 3456)), out((16, 1024)), out((16, 6912)), out((64, 256)),
            out((8, 6912)),
        ),
        name="finish",
    )(*done)
    decoded, *grads = results
    return (decoded.reshape(1, 2, 8, 8, 128), *(g.T for g in grads))


def solution(mesh):
    crops = P("section", "space", None, None, None)
    return jax.shard_map(
        body,
        mesh=mesh,
        in_specs=(crops, P(), P(), P(), P(), P(), P(), crops),
        out_specs=(crops, *([P(None, "space")] * 6)),
        check_vma=False,
    )
```

```python
import math

import jax
import jax.numpy as jnp
from jax import lax
from jax.experimental import pallas as pl
from jax.experimental.pallas import tpu as pltpu
from jax.sharding import PartitionSpec as P

BF = jnp.bfloat16
F32 = jnp.float32
MESH = pl.DeviceIdType.MESH
T = 128
GROUPS = ((0, 16), (16, 16), (32, 16), (48, 16), (64, 24), (88, 24), (112, 8))
UP_AT, BOTTOM_AT, JOIN_AT, DOWN_AT, ENC_AT, FIRST_AT = 0, 8, 62, 89, 97, 112
PADS = ((111, 112), (119, 120))
COLS = 120 * T
HALF, EIGHTH = COLS // 2, COLS // 8
FLOWS = (
    (0, "A", 0, 2, "bbd"),
    (1, "A", 0, 2, "bbd"),
    (2, "X", 0, 2, "bbd"),
    (3, "A", 0, 1, "bdd"),
    (3, "X", 1, 1, "bdd"),
    (4, "A", 0, 2, "bbd"),
    (4, "X", 2, 1, "bbd"),
    (5, "A", 0, 2, "bdd"),
    (5, "X", 2, 1, "bdd"),
    (6, "A", 0, 1, "bdd"),
)


def mm(a, b):
    return jnp.dot(a, b, preferred_element_type=F32)


def mm_t(a, b):
    return lax.dot_general(a, b, (((1,), (1,)), ((), ())), preferred_element_type=F32)


def silu(z):
    return z * jax.nn.sigmoid(z)


def slope(z):
    s = jax.nn.sigmoid(z)
    return s * (1.0 + z * (1.0 - s))


def one_hot(cond):
    return jnp.where(cond, 1.0, 0.0).astype(BF)


def iotas(shape):
    return lax.broadcasted_iota(jnp.int32, shape, 0), lax.broadcasted_iota(jnp.int32, shape, 1)


def block_row(v):
    y, z = (v >> 3) & 7, v & 7
    return ((v >> 6) * 4 + (y & 1) * 2 + (z & 1)) * 16 + (y >> 1) * 4 + (z >> 1)


def ds(at, size):
    return pl.ds(pl.multiple_of(at, T), size)


def kernel(
    vol_h, wf_h, we_h, wd_h, wb_h, wu_h, wj_h, cot_h,
    dec_o, full_o,
    vol, wf, we, wd, wb, wu, wj, cot, load_sem,
    shift, shift_c, perm, perm_t, eye, half_mask,
    wx, b_v, b_1, b_j, b_s, b_c, b_4, a_f, blocks, diag,
    z1, z2, e_skip,
    h1, sk, li, t7, t2, t4,
    h_vol, h_cot, h_t2, h_t4, h_send, h_recv,
    packed, r0, own, full,
    s0, q0, s4, q4, flows,
):
    sec, me = lax.axis_index("section"), lax.axis_index("space")
    core, my_x = sec % 2, sec // 2
    my_z, my_y = me // 4, me % 4

    loads = []
    for i, (src, dst) in enumerate(
        ((vol_h, vol), (wf_h, wf), (we_h, we), (wd_h, wd), (wb_h, wb), (wu_h, wu), (cot_h, cot), (wj_h, wj))
    ):
        copy = pltpu.make_async_copy(src, dst, load_sem.at[i])
        copy.start()
        loads.append(copy)
    l_vol, l_wf, l_we, l_wd, l_wb, l_wu, l_cot, l_wj = loads

    around = {d: (sec, (me + 16 + d) % 16) for d in (-3, -2, -1, 1, 2, 3)}
    after, before = around[1], around[-1]
    other_core = (sec + 1 - 2 * core, me)
    y_peers = [(sec, my_z * 4 + (my_y + d) % 4) for d in (1, 2, 3)]
    z_peers = [(sec, ((my_z + d) % 4) * 4 + my_y) for d in (1, 2, 3)]
    sec_peers = [((sec + d) % 8, me) for d in range(1, 8)]

    barrier = pltpu.get_barrier_semaphore()
    peers = [*around.values(), *y_peers, *z_peers, *sec_peers]
    for dev in peers:
        pl.semaphore_signal(barrier, inc=1, device_id=dev, device_id_type=MESH)

    r, c = iotas((64, 64))
    for k in range(9):
        oy, oz = k // 3 - 1, k % 3 - 1
        shift[k] = one_hot(((c >> 3) == (r >> 3) + oy) & ((c & 7) == (r & 7) + oz))
    r, c = iotas((16, 16))
    for k in range(9):
        oy, oz = k // 3 - 1, k % 3 - 1
        shift_c[k * 16 : (k + 1) * 16, :] = one_hot(((c >> 2) == (r >> 2) + oy) & ((c & 3) == (r & 3) + oz))
    r, c = iotas((T, T))
    perm[...] = one_hot(r == block_row(c))
    perm_t[...] = one_hot(c == block_row(r))
    half_mask[0] = one_hot(c < 64)
    half_mask[1] = one_hot(c >= 64)
    r, c = iotas((256, 256))
    eye[...] = one_hot(r == c)
    diag[...] = jnp.zeros((T, 2048), BF)
    for lo, hi in PADS:
        packed[:, :, lo * T : hi * T] = jnp.zeros((16, 16, (hi - lo) * T), BF)

    not_first = jnp.where(me > 0, 1.0, 0.0)
    not_last = jnp.where(me < 15, 1.0, 0.0)

    sends = []

    def remote(src, dst, send_sem, recv_sem, dev):
        return pltpu.make_async_remote_copy(
            src_ref=src, dst_ref=dst, send_sem=send_sem, recv_sem=recv_sem, device_id=dev, device_id_type=MESH
        )

    def push(index, src, dst, dev):
        copy = remote(src, dst, h_send.at[index], h_recv.at[index], dev)
        copy.start()
        sends.append(copy)
        return copy

    def swap(index, first, last, got):
        return push(index, last, got.at[0], after), push(index + 1, first, got.at[1], before)

    def arrived(pair, got):
        for copy in pair:
            copy.wait_recv()
        lo = (got[0].astype(F32) * not_first).astype(BF)
        hi = (got[1].astype(F32) * not_last).astype(BF)
        return lo, hi

    def inside(x, first, count, layer_rows):
        layer = lax.broadcasted_iota(jnp.int32, x.shape, 0) // layer_rows + first
        return jnp.where((layer >= 0) & (layer < count), x, 0.0).astype(BF)

    def spread(to, layers, row=0, per=2, width=T):
        step = per * 64 // 64
        for n in range(0, len(layers), step):
            group = layers[n : n + step]
            both = jnp.concatenate(group, axis=1)
            for k in range(9):
                moved = mm(shift[k], both).astype(BF)
                for m in range(len(group)):
                    to[row + (n + m) * 64 : row + (n + m + 1) * 64, k * width : (k + 1) * width] = (
                        moved[:, m * width : (m + 1) * width]
                    )

    def layers_of(x):
        return [x[i : i + 64] for i in range(0, x.shape[0], 64)]

    def spread_coarse(to, layers):
        moved = mm(shift_c[...], jnp.concatenate(layers, axis=1)).astype(BF)
        for n in range(len(layers)):
            for k in range(9):
                to[n * 16 : (n + 1) * 16, k * 256 : (k + 1) * 256] = (
                    moved[k * 16 : (k + 1) * 16, n * 256 : (n + 1) * 256]
                )

    def conv(b, w, count, rows):
        depth = b.shape[1]
        total = mm(b[0:count], w[0:depth, :])
        for ox in (1, 2):
            total = total + mm(b[ox * rows : ox * rows + count], w[ox * depth : (ox + 1) * depth, :])
        return total

    def conv_back(b, w, count, rows):
        cols = b.shape[1] // 9
        depth = w.shape[0] // 27
        total = jnp.zeros((count, depth), F32)
        for ox in range(3):
            for k in range(9):
                tap = ox * 9 + k
                total = total + mm_t(
                    b[(2 - ox) * rows : (2 - ox) * rows + count, (8 - k) * cols : (9 - k) * cols],
                    w[tap * depth : (tap + 1) * depth, :],
                )
        return total

    def stacked(flat):
        return jnp.concatenate([flat[:, t * T : (t + 1) * T] for t in range(8)], axis=0)

    def grad_128(step_t, part, tiles, half, chunk, tile, begin=0, end=None):
        width = chunk * T

        def piece(n):
            if n >= tiles:
                return jnp.zeros((16, 8, width), F32)
            return mm(step_t, part(n)).reshape(16, 8, width)

        for n in range(begin, end or half, chunk):
            at = (tile + n) * T
            packed[:, :, at : at + width] = jnp.concatenate([piece(n), piece(half + n)], axis=1).astype(BF)

    def grad_256(step_t, part, begin, end, tile):
        for n in range(begin, end, 2):
            at = (tile + n) * T
            packed[:, :, at : at + 256] = mm(step_t, part(n)).reshape(16, 16, 256).astype(BF)

    def turned(x):
        return mm_t(eye[0 : x.shape[1], 0 : x.shape[1]], x).astype(BF)

    def window(b, at, rows, count, chunk):
        per = b.shape[1] // T

        def part(n):
            ox, k = n // per, n % per
            begin = at + ox * rows
            return b[begin : begin + count, k * T : (k + chunk) * T]

        return part

    step_1, step_2 = 1 + 3 * core, 4 - 3 * core
    at_1 = my_y + core * (my_z - my_y)
    at_2 = my_z + core * (my_y - my_z)
    crossing, gathering = {}, {}

    def cross(g):
        first, n = GROUPS[g]
        w = n // 2 * T
        copy = remote(
            packed.at[:, :, ds(first * T + (1 - core) * w, w)],
            r0.at[:, :, pl.ds(first // 2 * T, w)],
            s0.at[g], q0.at[g], other_core,
        )
        copy.start()
        crossing[g] = copy
        sends.append(copy)

    def flow(f):
        g, kind, lo, tiles, how = FLOWS[f]
        refs = flows[f]
        first, n = GROUPS[g]
        e, w = n // 8, tiles * T
        coords = (at_1, at_2, my_x) if kind == "A" else (my_x, at_1, at_2)
        names = "12x" if kind == "A" else "x12"

        def dev(axis, v):
            if names[axis] == "1":
                return (sec, v * step_1 + at_2 * step_2)
            if names[axis] == "2":
                return (sec, at_1 * step_1 + v * step_2)
            return (v * 2 + core, me)

        def go(src, dst, sem, to):
            copy = remote(src, dst, refs["send"].at[sem], refs["recv"].at[sem], to)
            copy.start()
            sends.append(copy)
            return copy

        u = refs["u"][0]

        def build(i, carry):
            for j in range(4):
                p = i * step_1 + j * step_2
                for x in range(4):
                    at = (x * e + lo) * T
                    there = first // 2 * T + at
                    both = packed[p, :, ds(first * T + core * (n // 2 * T) + at, w)] + r0[p, :, there : there + w]
                    if kind == "A":
                        u[i, j * 4 + x] = both
                    else:
                        u[x, i * 4 + j] = both
            return carry

        lax.fori_loop(0, 4, build, 0)
        for axis in range(3):
            m_count = (16, 4, 1)[axis]
            c, u, r = coords[axis], refs["u"][axis], refs["r"][axis]
            sem = axis * 6

            def put(m, value):
                if axis < 2:
                    q = m_count // 4
                    refs["u"][axis + 1][m // q, m % q] = value
                else:
                    own[:, (first // 8 + lo) * T : (first // 8 + lo) * T + w] = value

            if how[axis] == "d":
                copies = [
                    go(u.at[(c + d) % 4], r.at[d - 1], sem + d - 1, dev(axis, (c + d) % 4)) for d in (1, 2, 3)
                ]
                yield
                for copy in copies:
                    copy.wait_recv()
                for m in range(m_count):
                    total = u[c, m].astype(F32)
                    for d in range(3):
                        total = total + r[d, m].astype(F32)
                    put(m, total.astype(BF))
                continue
            c1, c2, c3 = c + 1 - 2 * (c % 2), (c + 2) % 4, 3 - c
            h = m_count // 2
            low, high = pl.ds(0, h), pl.ds(h, h)
            keep, passed, got = refs["keep"][axis], refs["pass"][axis], refs["got"][axis]
            copies = [
                go(u.at[c1, low], r.at[0, low], sem, dev(axis, c1)),
                go(u.at[c3, high], r.at[0, high], sem + 1, dev(axis, c3)),
                go(u.at[c2, low], r.at[1, low], sem + 2, dev(axis, c1)),
                go(u.at[c2, high], r.at[1, high], sem + 3, dev(axis, c3)),
            ]
            yield
            for copy in copies:
                copy.wait_recv()
            for m in range(m_count):
                passed[m] = u[c3 if m < h else c1, m] + r[1, m]
            copies = [
                go(passed.at[low], got.at[low], sem + 4, dev(axis, c3)),
                go(passed.at[high], got.at[high], sem + 5, dev(axis, c1)),
            ]
            for m in range(m_count):
                keep[m] = u[c, m] + r[0, m]
            yield
            for copy in copies:
                copy.wait_recv()
            for m in range(m_count):
                put(m, keep[m] + got[m])

    running, finished = {}, set()

    def go_on(*which):
        for f in which:
            if f not in running:
                g = FLOWS[f][0]
                if g in crossing:
                    crossing.pop(g).wait_recv()
                running[f] = flow(f)
            if next(running[f], True):
                finished.add(f)

    def gather(g, everyone=False):
        first, n = GROUPS[g]
        q, at = n // 8 * T, first // 8 * T
        assert all(f in finished for f in range(len(FLOWS)) if FLOWS[f][0] == g)

        def copy_of(d, source):
            to = (sec + d) % 8 if everyone else (sec + 2 * d) % 8
            return remote(
                own.at[:, pl.ds(at, q)], full.at[:, ds(place_of(source), q)],
                s4.at[g, d - 1], q4.at[g, d - 1], (to, me),
            )

        def place_of(source):
            return first * T + source % 2 * (n // 2 * T) + source // 2 * q

        gathering[g] = []
        for d in range(1, 8) if everyone else (1, 2, 3):
            copy = copy_of(d, sec)
            copy.start()
            sends.append(copy)
            gathering[g].append(copy_of(d, (sec + 8 - (d if everyone else 2 * d)) % 8))
        full[:, ds(place_of(sec), q)] = own[:, at : at + q]

    def share(g):
        first, n = GROUPS[g]
        w = n // 2 * T
        for copy in gathering[g]:
            copy.wait_recv()

        def copy_of(c):
            where = full.at[:, ds(first * T + c * w, w)]
            return remote(where, where, s4.at[g, 7], q4.at[g, 7], other_core)

        copy = copy_of(core)
        copy.start()
        sends.append(copy)
        gathering[g] = [copy_of(1 - core)]

    l_vol.wait()
    l_cot.wait()
    pl.semaphore_wait(barrier, len(peers))
    pushed = {}
    for n, d in enumerate((1, -1, 2, -2, 3, -3)):
        pushed[-d] = push(n, vol, h_vol.at[3 - d], around[d])
    cot_pair = swap(6, cot.at[pl.ds(0, 64)], cot.at[pl.ds(64, 64)], h_cot)
    r, c = iotas((64, T))
    twice = one_hot(r == (c & 63))
    l_wf.wait()
    zero = jnp.zeros((64, T), BF)
    for tap in range(27):
        wx[tap * T : tap * T + 64, :] = wf[tap * 64 : (tap + 1) * 64, :]
        wx[tap * T + 64 : (tap + 1) * T, :] = zero
    spread(b_v, layers_of(mm(vol[...], twice).astype(BF)), 6 * 64)
    for d in (-1, 1, -2, 2, -3, 3):
        pushed[d].wait_recv()
        got = inside(mm(h_vol[3 + d], twice), 2 * (me + d), 32, 64)
        spread(b_v, layers_of(got), (3 + d) * T)
    z1_all = conv(b_v, wx, 768, 64)
    z1[...] = z1_all[320:448]
    h1[...] = inside(silu(z1_all), 2 * me - 5, 32, 64)
    spread(b_1, layers_of(h1))
    l_we.wait()
    z2_all = conv(b_1, we, 640, 64)
    z2[...] = z2_all[256:384]
    sk[...] = inside(silu(z2_all), 2 * me - 4, 32, 64)
    for n in range(5):
        moved = mm(perm[...], sk[n * T : (n + 1) * T]).astype(BF)
        for t in range(8):
            blocks[n * 16 : (n + 1) * 16, t * T : (t + 1) * T] = moved[t * 16 : (t + 1) * 16]
    l_wd.wait()
    z3 = mm(blocks[...], wd[...])
    g1 = silu(z3).astype(BF)
    spread_coarse(b_c, [g1[n * 16 : (n + 1) * 16] for n in range(5)])
    l_wb.wait()
    z4 = conv(b_c, wb, 48, 16)
    g2 = inside(silu(z4), me - 1, 16, 16)
    l_wu.wait()
    lifted = mm(g2, wu[...]).astype(BF)
    for n in range(3):
        li[n * T : (n + 1) * T] = mm(perm_t[...], stacked(lifted[n * 16 : (n + 1) * 16])).astype(BF)
    layers = [
        jnp.concatenate([li[n * 64 : (n + 1) * 64], sk[(n + 2) * 64 : (n + 3) * 64]], axis=1) for n in range(6)
    ]
    spread(b_j, layers, 0, 1, 256)
    l_wj.wait()
    z7 = conv(b_j, wj, 256, 64)
    dec_o[...] = silu(z7[64:192]).astype(BF)

    lo, hi = arrived(cot_pair, h_cot)
    cots = jnp.concatenate([lo, cot[...], hi], axis=0)
    t7[...] = (cots.astype(F32) * slope(z7)).astype(BF)
    spread(b_s, layers_of(t7))
    back = conv_back(b_s, wj, T, 64)
    e_skip[...] = back[:, T:256]
    moved = mm(perm[...], back[:, 0:T].astype(BF)).astype(BF)
    lift_blocks = jnp.concatenate([moved[t * 16 : (t + 1) * 16] for t in range(8)], axis=1)
    e3 = mm_t(lift_blocks, wu[...]).astype(BF)
    t4[...] = (e3.astype(F32) * slope(z4[16:32])).astype(BF)
    pair = swap(8, t4, t4, h_t4)
    for t in range(8):
        diag[t * 16 : (t + 1) * 16, t * 256 : (t + 1) * 256] = g2[16:32]
    moved_t = turned(moved)
    for t in range(8):
        up = mm(moved_t, diag[:, t * 256 : (t + 1) * 256]).astype(BF)
        for b in range(8):
            at = UP_AT * T + (b % 4) * 256
            packed[2 * t + b // 4, :, at : at + 256] = up[b * 16 : (b + 1) * 16]
    step_t = turned(t4[...])
    grad_256(step_t, window(b_c, 16, 16, 16, 2), 0, 8, BOTTOM_AT)
    cross(0)
    grad_256(step_t, window(b_c, 16, 16, 16, 2), 8, 24, BOTTOM_AT)
    cross(1)
    grad_256(step_t, window(b_c, 16, 16, 16, 2), 24, 40, BOTTOM_AT)
    cross(2)
    grad_256(step_t, window(b_c, 16, 16, 16, 2), 40, 54, BOTTOM_AT)
    step_t = turned(t7[64:192])
    grad_128(step_t, window(b_j, 64, 64, T, 3), 54, 27, 3, JOIN_AT, 0, 3)
    cross(3)
    grad_128(step_t, window(b_j, 64, 64, T, 3), 54, 27, 3, JOIN_AT, 3, 27)
    cross(4)
    go_on(0)
    lo, hi = arrived(pair, h_t4)
    spread_coarse(b_4, [lo, t4[...], hi])
    e4 = conv_back(b_4, wb, 16, 16).astype(BF)
    t3 = (e4.astype(F32) * slope(z3[32:48])).astype(BF)
    e5 = stacked(mm_t(t3, wd[...]))
    high = e5.astype(BF)
    low = (e5 - high.astype(F32)).astype(BF)
    e5 = mm(perm_t[...], high) + mm(perm_t[...], low)
    t2[...] = ((e5 + e_skip[...]) * slope(z2[...])).astype(BF)
    pair = swap(10, t2.at[pl.ds(0, 64)], t2.at[pl.ds(64, 64)], h_t2)
    go_on(1, 2, 4, 3)
    grad_256(turned(t3), lambda n: blocks[32:48, n * T : (n + 2) * T], 0, 8, DOWN_AT)
    grad_128(turned(t2[...]), window(b_1, 256, 64, T, 1), 27, 14, 1, ENC_AT)
    cross(5)
    go_on(6, 5, 0)
    spread(b_s, layers_of(t2), 64)
    lo, hi = arrived(pair, h_t2)
    spread(b_s, [lo], 0)
    spread(b_s, [hi], 192)
    back = conv_back(b_s, we, T, 64)
    t1 = (back.astype(BF).astype(F32) * slope(z1[...])).astype(BF)
    go_on(1)
    for j in range(14):
        left, right = (b_v[320 + t // 9 * 64 : 448 + t // 9 * 64, t % 9 * T : (t % 9 + 1) * T] for t in (2 * j, min(2 * j + 1, 26)))
        tile = left * half_mask[0]
        if j < 13:
            tile = tile + right * half_mask[1]
        a_f[:, j * T : (j + 1) * T] = tile
    grad_128(turned(t1), lambda n: a_f[:, n * T : (n + 1) * T], 14, 7, 1, FIRST_AT)
    cross(6)
    go_on(7, 8, 3, 2, 5, 0, 9, 1, 4, 6, 7, 8, 3, 5, 0, 2, 9, 1, 4, 6, 7, 8, 5, 0, 3, 2, 1, 9, 6, 4, 7, 0, 8)
    gather(0)
    go_on(5, 2, 1)
    gather(1)
    go_on(3, 9, 6, 4)
    gather(3)
    go_on(7, 8)
    gather(5)
    go_on(2)
    gather(2)
    go_on(5, 6)
    gather(4)
    go_on(9)
    gather(6, True)
    share(0)
    share(5)
    share(3)
    share(1)
    share(2)
    share(4)
    for g in (0, 1, 2, 3, 4, 5, 6):
        first, n = GROUPS[g]
        for copy in gathering[g]:
            copy.wait_recv()
        full_o[:, first * T : (first + n) * T] = full[:, first * T : (first + n) * T]
    for copy in sends:
        copy.wait_send()


def finish(dec, full, dec_o, gf_o, ge_o, gd_o, gb_o, gu_o, gj_o):
    factor = 1.0 / math.sqrt(16384)
    dec_o[...] = dec[...]

    def rows(tile, width):
        return full[:, tile * T : tile * T + width].astype(F32) * factor

    both = rows(JOIN_AT, 3456)
    gj_o[:, 0:3456] = both[0:8]
    gj_o[:, 3456:6912] = both[8:16]
    for b in range(4):
        gu_o[b * 16 : (b + 1) * 16, :] = rows(UP_AT + 2 * b, 256)
    gb_o[...] = rows(BOTTOM_AT, 6912)
    gd_o[...] = rows(DOWN_AT, 1024)
    both = rows(ENC_AT, 1792)
    ge_o[:, 0:1792] = both[0:8]
    ge_o[:, 1792:3456] = both[8:16, 0:1664]
    both = rows(FIRST_AT, 896)
    gf_o[:, 0:896] = both[0:8]
    gf_o[:, 896:1728] = both[8:16, 0:832]


def flow_scratch(tiles, how):
    v, w = lambda *shape: pltpu.VMEM((*shape, 16, tiles * T), BF), (16, 4, 1)
    two = [how[i] == "b" for i in range(3)]
    return {
        "u": [v(4, m) for m in w],
        "r": [v(2 if two[i] else 3, m) for i, m in enumerate(w)],
        **{name: [v(m) if two[i] else v(1) for i, m in enumerate(w)] for name in ("keep", "pass", "got")},
        "send": pltpu.SemaphoreType.DMA((18,)),
        "recv": pltpu.SemaphoreType.DMA((18,)),
    }


def scratch():
    v, dma = pltpu.VMEM, pltpu.SemaphoreType.DMA
    return [
        v((128, 64), BF), v((1728, 128), BF), v((3456, 128), BF), v((1024, 256), BF), v((6912, 256), BF),
        v((256, 1024), BF), v((6912, 128), BF), v((128, 128), BF), dma((8,)),
        v((9, 64, 64), BF), v((144, 16), BF), v((T, T), BF), v((T, T), BF), v((256, 256), BF), v((2, T, T), BF),
        v((3456, T), BF), v((896, 1152), BF), v((768, 1152), BF), v((384, 2304), BF), v((256, 1152), BF),
        v((80, 2304), BF), v((48, 2304), BF), v((T, 1792), BF), v((80, 1024), BF), v((T, 2048), BF),
        v((T, T), F32), v((T, T), F32), v((T, T), F32),
        v((768, T), BF), v((640, T), BF), v((384, T), BF), v((256, T), BF), v((T, T), BF), v((16, 256), BF),
        v((7, T, 64), BF), v((2, 64, T), BF), v((2, 64, T), BF), v((2, 16, 256), BF), dma((12,)), dma((12,)),
        v((16, 16, COLS), BF), v((16, 16, HALF), BF), v((16, EIGHTH), BF), v((16, COLS), BF),
        dma((8,)), dma((8,)), dma((8, 8)), dma((8, 8)), [flow_scratch(*f[3:]) for f in FLOWS],
    ]


def body(volume, w_first, w_enc, w_down, w_bottom, w_up, w_join, cotangent):
    out = lambda shape, dtype=F32: jax.ShapeDtypeStruct(shape, dtype)
    done = pl.pallas_call(
        kernel,
        out_shape=(out((128, 128), BF), out((16, COLS), BF)),
        in_specs=[pl.BlockSpec(memory_space=pl.ANY)] * 8,
        out_specs=[pl.BlockSpec(memory_space=pltpu.VMEM)] * 2,
        scratch_shapes=scratch(),
        compiler_params=pltpu.CompilerParams(
            collective_id=0, has_side_effects=True, vmem_limit_bytes=58 * 1024 * 1024
        ),
        name="step",
    )(
        volume.reshape(128, 64), w_first, w_enc, w_down, w_bottom, w_up, w_join, cotangent.reshape(128, 128)
    )
    results = pl.pallas_call(
        finish,
        out_shape=(
            out((128, 128), BF), out((8, 1728)), out((8, 3456)), out((16, 1024)), out((16, 6912)), out((64, 256)),
            out((8, 6912)),
        ),
        name="finish",
    )(*done)
    decoded, *grads = results
    return (decoded.reshape(1, 2, 8, 8, 128), *(g.T for g in grads))


def solution(mesh):
    crops = P("section", "space", None, None, None)
    return jax.shard_map(
        body,
        mesh=mesh,
        in_specs=(crops, P(), P(), P(), P(), P(), P(), crops),
        out_specs=(crops, *([P(None, "space")] * 6)),
        check_vma=False,
    )
```

```python
import math

import jax
import jax.numpy as jnp
from jax import lax
from jax.experimental import pallas as pl
from jax.experimental.pallas import tpu as pltpu
from jax.sharding import PartitionSpec as P

BF = jnp.bfloat16
F32 = jnp.float32
MESH = pl.DeviceIdType.MESH
T = 128
GROUPS = ((0, 16), (16, 16), (32, 16), (48, 16), (64, 24), (88, 24), (112, 8))
UP_AT, BOTTOM_AT, JOIN_AT, DOWN_AT, ENC_AT, FIRST_AT = 0, 8, 62, 89, 97, 112
PADS = ((111, 112), (119, 120))
COLS = 120 * T
HALF, EIGHTH = COLS // 2, COLS // 8
FLOWS = (
    (0, "A", 0, 2, "bbd"),
    (1, "A", 0, 2, "bbd"),
    (2, "A", 0, 1, "bdd"),
    (2, "X", 1, 1, "bdd"),
    (3, "A", 0, 2, "bdd"),
    (4, "A", 0, 1, "bdd"),
    (4, "X", 1, 2, "bdd"),
    (5, "A", 0, 2, "bdd"),
    (5, "X", 2, 1, "bdd"),
    (6, "A", 0, 1, "bdd"),
)


def mm(a, b):
    return jnp.dot(a, b, preferred_element_type=F32)


def mm_t(a, b):
    return lax.dot_general(a, b, (((1,), (1,)), ((), ())), preferred_element_type=F32)


def silu(z):
    return z * jax.nn.sigmoid(z)


def slope(z):
    s = jax.nn.sigmoid(z)
    return s * (1.0 + z * (1.0 - s))


def one_hot(cond):
    return jnp.where(cond, 1.0, 0.0).astype(BF)


def iotas(shape):
    return lax.broadcasted_iota(jnp.int32, shape, 0), lax.broadcasted_iota(jnp.int32, shape, 1)


def block_row(v):
    y, z = (v >> 3) & 7, v & 7
    return ((v >> 6) * 4 + (y & 1) * 2 + (z & 1)) * 16 + (y >> 1) * 4 + (z >> 1)


def ds(at, size):
    return pl.ds(pl.multiple_of(at, T), size)


def kernel(
    vol_h, wf_h, we_h, wd_h, wb_h, wu_h, wj_h, cot_h,
    dec_o, full_o,
    vol, wf, we, wd, wb, wu, wj, cot, load_sem,
    shift, shift_c, perm, perm_t, eye, half_mask,
    wx, b_v, b_1, b_j, b_s, b_c, b_4, a_f, blocks, diag,
    z1, z2, e_skip,
    h1, sk, li, t7, t2, t4,
    h_vol, h_cot, h_t2, h_t4, h_send, h_recv,
    packed, r0, own, full,
    s0, q0, s4, q4, flows,
):
    sec, me = lax.axis_index("section"), lax.axis_index("space")
    core, my_x = sec % 2, sec // 2
    my_z, my_y = me // 4, me % 4

    loads = []
    for i, (src, dst) in enumerate(
        ((vol_h, vol), (wf_h, wf), (we_h, we), (wd_h, wd), (wb_h, wb), (wu_h, wu), (cot_h, cot), (wj_h, wj))
    ):
        copy = pltpu.make_async_copy(src, dst, load_sem.at[i])
        copy.start()
        loads.append(copy)
    l_vol, l_wf, l_we, l_wd, l_wb, l_wu, l_cot, l_wj = loads

    around = {d: (sec, (me + 16 + d) % 16) for d in (-3, -2, -1, 1, 2, 3)}
    after, before = around[1], around[-1]
    other_core = (sec + 1 - 2 * core, me)
    y_peers = [(sec, my_z * 4 + (my_y + d) % 4) for d in (1, 2, 3)]
    z_peers = [(sec, ((my_z + d) % 4) * 4 + my_y) for d in (1, 2, 3)]
    sec_peers = [((sec + d) % 8, me) for d in range(1, 8)]

    barrier = pltpu.get_barrier_semaphore()
    peers = [*around.values(), *y_peers, *z_peers, *sec_peers]
    for dev in peers:
        pl.semaphore_signal(barrier, inc=1, device_id=dev, device_id_type=MESH)

    r, c = iotas((64, 64))
    for k in range(9):
        oy, oz = k // 3 - 1, k % 3 - 1
        shift[k] = one_hot(((c >> 3) == (r >> 3) + oy) & ((c & 7) == (r & 7) + oz))
    r, c = iotas((16, 16))
    for k in range(9):
        oy, oz = k // 3 - 1, k % 3 - 1
        shift_c[k * 16 : (k + 1) * 16, :] = one_hot(((c >> 2) == (r >> 2) + oy) & ((c & 3) == (r & 3) + oz))
    r, c = iotas((T, T))
    perm[...] = one_hot(r == block_row(c))
    perm_t[...] = one_hot(c == block_row(r))
    half_mask[0] = one_hot(c < 64)
    half_mask[1] = one_hot(c >= 64)
    r, c = iotas((256, 256))
    eye[...] = one_hot(r == c)
    diag[...] = jnp.zeros((T, 2048), BF)
    for lo, hi in PADS:
        packed[:, :, lo * T : hi * T] = jnp.zeros((16, 16, (hi - lo) * T), BF)

    not_first = jnp.where(me > 0, 1.0, 0.0)
    not_last = jnp.where(me < 15, 1.0, 0.0)

    sends = []

    def remote(src, dst, send_sem, recv_sem, dev):
        return pltpu.make_async_remote_copy(
            src_ref=src, dst_ref=dst, send_sem=send_sem, recv_sem=recv_sem, device_id=dev, device_id_type=MESH
        )

    def push(index, src, dst, dev):
        copy = remote(src, dst, h_send.at[index], h_recv.at[index], dev)
        copy.start()
        sends.append(copy)
        return copy

    def swap(index, first, last, got):
        return push(index, last, got.at[0], after), push(index + 1, first, got.at[1], before)

    def arrived(pair, got):
        for copy in pair:
            copy.wait_recv()
        lo = (got[0].astype(F32) * not_first).astype(BF)
        hi = (got[1].astype(F32) * not_last).astype(BF)
        return lo, hi

    def inside(x, first, count, layer_rows):
        layer = lax.broadcasted_iota(jnp.int32, x.shape, 0) // layer_rows + first
        return jnp.where((layer >= 0) & (layer < count), x, 0.0).astype(BF)

    def spread(to, layers, row=0, per=2, width=T):
        step = per * 64 // 64
        for n in range(0, len(layers), step):
            group = layers[n : n + step]
            both = jnp.concatenate(group, axis=1)
            for k in range(9):
                moved = mm(shift[k], both).astype(BF)
                for m in range(len(group)):
                    to[row + (n + m) * 64 : row + (n + m + 1) * 64, k * width : (k + 1) * width] = (
                        moved[:, m * width : (m + 1) * width]
                    )

    def layers_of(x):
        return [x[i : i + 64] for i in range(0, x.shape[0], 64)]

    def spread_coarse(to, layers):
        moved = mm(shift_c[...], jnp.concatenate(layers, axis=1)).astype(BF)
        for n in range(len(layers)):
            for k in range(9):
                to[n * 16 : (n + 1) * 16, k * 256 : (k + 1) * 256] = (
                    moved[k * 16 : (k + 1) * 16, n * 256 : (n + 1) * 256]
                )

    def conv(b, w, count, rows):
        depth = b.shape[1]
        total = mm(b[0:count], w[0:depth, :])
        for ox in (1, 2):
            total = total + mm(b[ox * rows : ox * rows + count], w[ox * depth : (ox + 1) * depth, :])
        return total

    def conv_back(b, w, count, rows):
        cols = b.shape[1] // 9
        depth = w.shape[0] // 27
        total = jnp.zeros((count, depth), F32)
        for ox in range(3):
            for k in range(9):
                tap = ox * 9 + k
                total = total + mm_t(
                    b[(2 - ox) * rows : (2 - ox) * rows + count, (8 - k) * cols : (9 - k) * cols],
                    w[tap * depth : (tap + 1) * depth, :],
                )
        return total

    def stacked(flat):
        return jnp.concatenate([flat[:, t * T : (t + 1) * T] for t in range(8)], axis=0)

    def grad_128(step_t, part, tiles, half, chunk, tile, begin=0, end=None):
        width = chunk * T

        def piece(n):
            if n >= tiles:
                return jnp.zeros((16, 8, width), F32)
            return mm(step_t, part(n)).reshape(16, 8, width)

        for n in range(begin, end or half, chunk):
            at = (tile + n) * T
            packed[:, :, at : at + width] = jnp.concatenate([piece(n), piece(half + n)], axis=1).astype(BF)

    def grad_256(step_t, part, begin, end, tile):
        for n in range(begin, end, 2):
            at = (tile + n) * T
            packed[:, :, at : at + 256] = mm(step_t, part(n)).reshape(16, 16, 256).astype(BF)

    def turned(x):
        return mm_t(eye[0 : x.shape[1], 0 : x.shape[1]], x).astype(BF)

    def window(b, at, rows, count, chunk):
        per = b.shape[1] // T

        def part(n):
            ox, k = n // per, n % per
            begin = at + ox * rows
            return b[begin : begin + count, k * T : (k + chunk) * T]

        return part

    step_1, step_2 = 1 + 3 * core, 4 - 3 * core
    at_1 = my_y + core * (my_z - my_y)
    at_2 = my_z + core * (my_y - my_z)
    crossing, gathering = {}, {}

    def cross(g):
        first, n = GROUPS[g]
        w = n // 2 * T
        copy = remote(
            packed.at[:, :, ds(first * T + (1 - core) * w, w)],
            r0.at[:, :, pl.ds(first // 2 * T, w)],
            s0.at[g], q0.at[g], other_core,
        )
        copy.start()
        crossing[g] = copy
        sends.append(copy)

    def flow(f):
        g, kind, lo, tiles, how = FLOWS[f]
        refs = flows[f]
        first, n = GROUPS[g]
        e, w = n // 8, tiles * T
        coords = (at_1, at_2, my_x) if kind == "A" else (my_x, at_1, at_2)
        names = "12x" if kind == "A" else "x12"

        def dev(axis, v):
            if names[axis] == "1":
                return (sec, v * step_1 + at_2 * step_2)
            if names[axis] == "2":
                return (sec, at_1 * step_1 + v * step_2)
            return (v * 2 + core, me)

        def go(src, dst, sem, to):
            copy = remote(src, dst, refs["send"].at[sem], refs["recv"].at[sem], to)
            copy.start()
            sends.append(copy)
            return copy

        u = refs["u"][0]

        def build(i, carry):
            for j in range(4):
                p = i * step_1 + j * step_2
                for x in range(4):
                    at = (x * e + lo) * T
                    there = first // 2 * T + at
                    both = packed[p, :, ds(first * T + core * (n // 2 * T) + at, w)] + r0[p, :, there : there + w]
                    if kind == "A":
                        u[i, j * 4 + x] = both
                    else:
                        u[x, i * 4 + j] = both
            return carry

        lax.fori_loop(0, 4, build, 0)
        for axis in range(3):
            m_count = (16, 4, 1)[axis]
            c, u, r = coords[axis], refs["u"][axis], refs["r"][axis]
            sem = axis * 6

            def put(m, value):
                if axis < 2:
                    q = m_count // 4
                    refs["u"][axis + 1][m // q, m % q] = value
                else:
                    own[:, (first // 8 + lo) * T : (first // 8 + lo) * T + w] = value

            if how[axis] == "d":
                copies = [
                    go(u.at[(c + d) % 4], r.at[d - 1], sem + d - 1, dev(axis, (c + d) % 4)) for d in (1, 2, 3)
                ]
                yield
                for copy in copies:
                    copy.wait_recv()
                for m in range(m_count):
                    total = u[c, m].astype(F32)
                    for d in range(3):
                        total = total + r[d, m].astype(F32)
                    put(m, total.astype(BF))
                continue
            c1, c2, c3 = c + 1 - 2 * (c % 2), (c + 2) % 4, 3 - c
            h = m_count // 2
            low, high = pl.ds(0, h), pl.ds(h, h)
            keep, passed, got = refs["keep"][axis], refs["pass"][axis], refs["got"][axis]
            copies = [
                go(u.at[c1, low], r.at[0, low], sem, dev(axis, c1)),
                go(u.at[c3, high], r.at[0, high], sem + 1, dev(axis, c3)),
                go(u.at[c2, low], r.at[1, low], sem + 2, dev(axis, c1)),
                go(u.at[c2, high], r.at[1, high], sem + 3, dev(axis, c3)),
            ]
            yield
            for copy in copies:
                copy.wait_recv()
            for m in range(m_count):
                passed[m] = u[c3 if m < h else c1, m] + r[1, m]
            copies = [
                go(passed.at[low], got.at[low], sem + 4, dev(axis, c3)),
                go(passed.at[high], got.at[high], sem + 5, dev(axis, c1)),
            ]
            for m in range(m_count):
                keep[m] = u[c, m] + r[0, m]
            yield
            for copy in copies:
                copy.wait_recv()
            for m in range(m_count):
                put(m, keep[m] + got[m])

    running, finished = {}, set()

    def go_on(*which):
        for f in which:
            if f not in running:
                g = FLOWS[f][0]
                if g in crossing:
                    crossing.pop(g).wait_recv()
                running[f] = flow(f)
            if next(running[f], True):
                finished.add(f)

    def gather(g, everyone=False):
        first, n = GROUPS[g]
        q, at = n // 8 * T, first // 8 * T
        assert all(f in finished for f in range(len(FLOWS)) if FLOWS[f][0] == g)

        def copy_of(d, source):
            to = (sec + d) % 8 if everyone else (sec + 2 * d) % 8
            return remote(
                own.at[:, pl.ds(at, q)], full.at[:, ds(place_of(source), q)],
                s4.at[g, d - 1], q4.at[g, d - 1], (to, me),
            )

        def place_of(source):
            return first * T + source % 2 * (n // 2 * T) + source // 2 * q

        gathering[g] = []
        for d in range(1, 8) if everyone else (1, 2, 3):
            copy = copy_of(d, sec)
            copy.start()
            sends.append(copy)
            gathering[g].append(copy_of(d, (sec + 8 - (d if everyone else 2 * d)) % 8))
        full[:, ds(place_of(sec), q)] = own[:, at : at + q]

    def share(g):
        first, n = GROUPS[g]
        w = n // 2 * T
        for copy in gathering[g]:
            copy.wait_recv()

        def copy_of(c):
            where = full.at[:, ds(first * T + c * w, w)]
            return remote(where, where, s4.at[g, 7], q4.at[g, 7], other_core)

        copy = copy_of(core)
        copy.start()
        sends.append(copy)
        gathering[g] = [copy_of(1 - core)]

    l_vol.wait()
    l_cot.wait()
    pl.semaphore_wait(barrier, len(peers))
    pushed = {}
    for n, d in enumerate((1, -1, 2, -2, 3, -3)):
        pushed[-d] = push(n, vol, h_vol.at[3 - d], around[d])
    cot_pair = swap(6, cot.at[pl.ds(0, 64)], cot.at[pl.ds(64, 64)], h_cot)
    r, c = iotas((64, T))
    twice = one_hot(r == (c & 63))
    l_wf.wait()
    zero = jnp.zeros((64, T), BF)
    for tap in range(27):
        wx[tap * T : tap * T + 64, :] = wf[tap * 64 : (tap + 1) * 64, :]
        wx[tap * T + 64 : (tap + 1) * T, :] = zero
    spread(b_v, layers_of(mm(vol[...], twice).astype(BF)), 6 * 64)
    for d in (-1, 1, -2, 2, -3, 3):
        pushed[d].wait_recv()
        got = inside(mm(h_vol[3 + d], twice), 2 * (me + d), 32, 64)
        spread(b_v, layers_of(got), (3 + d) * T)
    z1_all = conv(b_v, wx, 768, 64)
    z1[...] = z1_all[320:448]
    h1[...] = inside(silu(z1_all), 2 * me - 5, 32, 64)
    spread(b_1, layers_of(h1))
    l_we.wait()
    z2_all = conv(b_1, we, 640, 64)
    z2[...] = z2_all[256:384]
    sk[...] = inside(silu(z2_all), 2 * me - 4, 32, 64)
    for n in range(5):
        moved = mm(perm[...], sk[n * T : (n + 1) * T]).astype(BF)
        for t in range(8):
            blocks[n * 16 : (n + 1) * 16, t * T : (t + 1) * T] = moved[t * 16 : (t + 1) * 16]
    l_wd.wait()
    z3 = mm(blocks[...], wd[...])
    g1 = silu(z3).astype(BF)
    spread_coarse(b_c, [g1[n * 16 : (n + 1) * 16] for n in range(5)])
    l_wb.wait()
    z4 = conv(b_c, wb, 48, 16)
    g2 = inside(silu(z4), me - 1, 16, 16)
    l_wu.wait()
    lifted = mm(g2, wu[...]).astype(BF)
    for n in range(3):
        li[n * T : (n + 1) * T] = mm(perm_t[...], stacked(lifted[n * 16 : (n + 1) * 16])).astype(BF)
    layers = [
        jnp.concatenate([li[n * 64 : (n + 1) * 64], sk[(n + 2) * 64 : (n + 3) * 64]], axis=1) for n in range(6)
    ]
    spread(b_j, layers, 0, 1, 256)
    l_wj.wait()
    z7 = conv(b_j, wj, 256, 64)
    dec_o[...] = silu(z7[64:192]).astype(BF)

    lo, hi = arrived(cot_pair, h_cot)
    cots = jnp.concatenate([lo, cot[...], hi], axis=0)
    t7[...] = (cots.astype(F32) * slope(z7)).astype(BF)
    spread(b_s, layers_of(t7))
    back = conv_back(b_s, wj, T, 64)
    e_skip[...] = back[:, T:256]
    moved = mm(perm[...], back[:, 0:T].astype(BF)).astype(BF)
    lift_blocks = jnp.concatenate([moved[t * 16 : (t + 1) * 16] for t in range(8)], axis=1)
    e3 = mm_t(lift_blocks, wu[...]).astype(BF)
    t4[...] = (e3.astype(F32) * slope(z4[16:32])).astype(BF)
    pair = swap(8, t4, t4, h_t4)
    for t in range(8):
        diag[t * 16 : (t + 1) * 16, t * 256 : (t + 1) * 256] = g2[16:32]
    moved_t = turned(moved)
    for t in range(8):
        up = mm(moved_t, diag[:, t * 256 : (t + 1) * 256]).astype(BF)
        for b in range(8):
            at = UP_AT * T + (b % 4) * 256
            packed[2 * t + b // 4, :, at : at + 256] = up[b * 16 : (b + 1) * 16]
    step_t = turned(t4[...])
    grad_256(step_t, window(b_c, 16, 16, 16, 2), 0, 8, BOTTOM_AT)
    cross(0)
    grad_256(step_t, window(b_c, 16, 16, 16, 2), 8, 24, BOTTOM_AT)
    cross(1)
    grad_256(step_t, window(b_c, 16, 16, 16, 2), 24, 40, BOTTOM_AT)
    cross(2)
    grad_256(step_t, window(b_c, 16, 16, 16, 2), 40, 54, BOTTOM_AT)
    step_t = turned(t7[64:192])
    grad_128(step_t, window(b_j, 64, 64, T, 3), 54, 27, 3, JOIN_AT, 0, 3)
    cross(3)
    grad_128(step_t, window(b_j, 64, 64, T, 3), 54, 27, 3, JOIN_AT, 3, 27)
    cross(4)
    go_on(0)
    lo, hi = arrived(pair, h_t4)
    spread_coarse(b_4, [lo, t4[...], hi])
    e4 = conv_back(b_4, wb, 16, 16).astype(BF)
    t3 = (e4.astype(F32) * slope(z3[32:48])).astype(BF)
    e5 = stacked(mm_t(t3, wd[...]))
    high = e5.astype(BF)
    low = (e5 - high.astype(F32)).astype(BF)
    e5 = mm(perm_t[...], high) + mm(perm_t[...], low)
    t2[...] = ((e5 + e_skip[...]) * slope(z2[...])).astype(BF)
    pair = swap(10, t2.at[pl.ds(0, 64)], t2.at[pl.ds(64, 64)], h_t2)
    go_on(1, 3, 2, 4)
    grad_256(turned(t3), lambda n: blocks[32:48, n * T : (n + 2) * T], 0, 8, DOWN_AT)
    grad_128(turned(t2[...]), window(b_1, 256, 64, T, 1), 27, 14, 1, ENC_AT)
    cross(5)
    go_on(5, 6, 0)
    spread(b_s, layers_of(t2), 64)
    lo, hi = arrived(pair, h_t2)
    spread(b_s, [lo], 0)
    spread(b_s, [hi], 192)
    back = conv_back(b_s, we, T, 64)
    t1 = (back.astype(BF).astype(F32) * slope(z1[...])).astype(BF)
    for j in range(14):
        left, right = (b_v[320 + t // 9 * 64 : 448 + t // 9 * 64, t % 9 * T : (t % 9 + 1) * T] for t in (2 * j, min(2 * j + 1, 26)))
        tile = left * half_mask[0]
        if j < 13:
            tile = tile + right * half_mask[1]
        a_f[:, j * T : (j + 1) * T] = tile
    grad_128(turned(t1), lambda n: a_f[:, n * T : (n + 1) * T], 14, 7, 1, FIRST_AT)
    cross(6)
    go_on(1, 7, 3, 8, 2, 4, 9, 5, 0, 6, 1, 3, 7, 8, 2, 4, 9, 5, 0, 6, 1, 3, 7, 8, 2, 4, 9, 5, 0, 6, 1, 3, 2, 7, 4)
    gather(3)
    go_on(8)
    gather(2)
    go_on(9, 5, 0)
    gather(0)
    go_on(6)
    gather(4)
    go_on(1)
    gather(1)
    go_on(7, 8)
    gather(5, True)
    share(2)
    go_on(9)
    gather(6, True)
    share(3)
    share(0)
    share(1)
    share(4)
    for g in (0, 1, 2, 3, 4, 5, 6):
        first, n = GROUPS[g]
        for copy in gathering[g]:
            copy.wait_recv()
        full_o[:, first * T : (first + n) * T] = full[:, first * T : (first + n) * T]
    for copy in sends:
        copy.wait_send()


def finish(dec, full, dec_o, gf_o, ge_o, gd_o, gb_o, gu_o, gj_o):
    factor = 1.0 / math.sqrt(16384)
    dec_o[...] = dec[...]

    def rows(tile, width):
        return full[:, tile * T : tile * T + width].astype(F32) * factor

    both = rows(JOIN_AT, 3456)
    gj_o[:, 0:3456] = both[0:8]
    gj_o[:, 3456:6912] = both[8:16]
    for b in range(4):
        gu_o[b * 16 : (b + 1) * 16, :] = rows(UP_AT + 2 * b, 256)
    gb_o[...] = rows(BOTTOM_AT, 6912)
    gd_o[...] = rows(DOWN_AT, 1024)
    both = rows(ENC_AT, 1792)
    ge_o[:, 0:1792] = both[0:8]
    ge_o[:, 1792:3456] = both[8:16, 0:1664]
    both = rows(FIRST_AT, 896)
    gf_o[:, 0:896] = both[0:8]
    gf_o[:, 896:1728] = both[8:16, 0:832]


def flow_scratch(tiles, how):
    v, w = lambda *shape: pltpu.VMEM((*shape, 16, tiles * T), BF), (16, 4, 1)
    two = [how[i] == "b" for i in range(3)]
    return {
        "u": [v(4, m) for m in w],
        "r": [v(2 if two[i] else 3, m) for i, m in enumerate(w)],
        **{name: [v(m) if two[i] else v(1) for i, m in enumerate(w)] for name in ("keep", "pass", "got")},
        "send": pltpu.SemaphoreType.DMA((18,)),
        "recv": pltpu.SemaphoreType.DMA((18,)),
    }


def scratch():
    v, dma = pltpu.VMEM, pltpu.SemaphoreType.DMA
    return [
        v((128, 64), BF), v((1728, 128), BF), v((3456, 128), BF), v((1024, 256), BF), v((6912, 256), BF),
        v((256, 1024), BF), v((6912, 128), BF), v((128, 128), BF), dma((8,)),
        v((9, 64, 64), BF), v((144, 16), BF), v((T, T), BF), v((T, T), BF), v((256, 256), BF), v((2, T, T), BF),
        v((3456, T), BF), v((896, 1152), BF), v((768, 1152), BF), v((384, 2304), BF), v((256, 1152), BF),
        v((80, 2304), BF), v((48, 2304), BF), v((T, 1792), BF), v((80, 1024), BF), v((T, 2048), BF),
        v((T, T), F32), v((T, T), F32), v((T, T), F32),
        v((768, T), BF), v((640, T), BF), v((384, T), BF), v((256, T), BF), v((T, T), BF), v((16, 256), BF),
        v((7, T, 64), BF), v((2, 64, T), BF), v((2, 64, T), BF), v((2, 16, 256), BF), dma((12,)), dma((12,)),
        v((16, 16, COLS), BF), v((16, 16, HALF), BF), v((16, EIGHTH), BF), v((16, COLS), BF),
        dma((8,)), dma((8,)), dma((8, 8)), dma((8, 8)), [flow_scratch(*f[3:]) for f in FLOWS],
    ]


def body(volume, w_first, w_enc, w_down, w_bottom, w_up, w_join, cotangent):
    out = lambda shape, dtype=F32: jax.ShapeDtypeStruct(shape, dtype)
    done = pl.pallas_call(
        kernel,
        out_shape=(out((128, 128), BF), out((16, COLS), BF)),
        in_specs=[pl.BlockSpec(memory_space=pl.ANY)] * 8,
        out_specs=[pl.BlockSpec(memory_space=pltpu.VMEM)] * 2,
        scratch_shapes=scratch(),
        compiler_params=pltpu.CompilerParams(
            collective_id=0, has_side_effects=True, vmem_limit_bytes=58 * 1024 * 1024
        ),
        name="step",
    )(
        volume.reshape(128, 64), w_first, w_enc, w_down, w_bottom, w_up, w_join, cotangent.reshape(128, 128)
    )
    results = pl.pallas_call(
        finish,
        out_shape=(
            out((128, 128), BF), out((8, 1728)), out((8, 3456)), out((16, 1024)), out((16, 6912)), out((64, 256)),
            out((8, 6912)),
        ),
        name="finish",
    )(*done)
    decoded, *grads = results
    return (decoded.reshape(1, 2, 8, 8, 128), *(g.T for g in grads))


def solution(mesh):
    crops = P("section", "space", None, None, None)
    return jax.shard_map(
        body,
        mesh=mesh,
        in_specs=(crops, P(), P(), P(), P(), P(), P(), crops),
        out_specs=(crops, *([P(None, "space")] * 6)),
        check_vma=False,
    )
```

```python
import math

import jax
import jax.numpy as jnp
from jax import lax
from jax.experimental import pallas as pl
from jax.experimental.pallas import tpu as pltpu
from jax.sharding import PartitionSpec as P

BF = jnp.bfloat16
F32 = jnp.float32
MESH = pl.DeviceIdType.MESH
T = 128
GROUPS = ((0, 16), (16, 16), (32, 16), (48, 16), (64, 24), (88, 24), (112, 8))
UP_AT, BOTTOM_AT, JOIN_AT, DOWN_AT, ENC_AT, FIRST_AT = 0, 8, 62, 89, 97, 112
PADS = ((111, 112), (119, 120))
COLS = 120 * T
HALF, EIGHTH = COLS // 2, COLS // 8
FLOWS = (
    (0, "A", 0, 2, "bbd"),
    (1, "A", 0, 2, "bbd"),
    (2, "A", 0, 1, "bdd"),
    (2, "X", 1, 1, "bdd"),
    (3, "A", 0, 2, "bdd"),
    (4, "A", 0, 1, "bdd"),
    (4, "X", 1, 2, "bdd"),
    (5, "A", 0, 2, "bdd"),
    (5, "X", 2, 1, "bdd"),
    (6, "A", 0, 1, "bdd"),
)


def mm(a, b):
    return jnp.dot(a, b, preferred_element_type=F32)


def mm_t(a, b):
    return lax.dot_general(a, b, (((1,), (1,)), ((), ())), preferred_element_type=F32)


def silu(z):
    return z * jax.nn.sigmoid(z)


def slope(z):
    s = jax.nn.sigmoid(z)
    return s * (1.0 + z * (1.0 - s))


def one_hot(cond):
    return jnp.where(cond, 1.0, 0.0).astype(BF)


def iotas(shape):
    return lax.broadcasted_iota(jnp.int32, shape, 0), lax.broadcasted_iota(jnp.int32, shape, 1)


def block_row(v):
    y, z = (v >> 3) & 7, v & 7
    return ((v >> 6) * 4 + (y & 1) * 2 + (z & 1)) * 16 + (y >> 1) * 4 + (z >> 1)


def ds(at, size):
    return pl.ds(pl.multiple_of(at, T), size)


def kernel(
    vol_h, wf_h, we_h, wd_h, wb_h, wu_h, wj_h, cot_h,
    dec_o, full_o,
    vol, wf, we, wd, wb, wu, wj, cot, load_sem,
    shift, shift_c, perm, perm_t, eye, half_mask,
    pairs, b_d, wx, b_v, b_1, b_j, b_s, b_c, b_4, a_f, blocks, diag,
    z1, z2, e_skip,
    h1, sk, li, t7, t2, t4,
    h_vol, h_cot, h_t2, h_t4, h_send, h_recv,
    packed, r0, own, full,
    s0, q0, s4, q4, flows,
):
    sec, me = lax.axis_index("section"), lax.axis_index("space")
    core, my_x = sec % 2, sec // 2
    my_z, my_y = me // 4, me % 4

    loads = []
    for i, (src, dst) in enumerate(
        ((vol_h, vol), (wf_h, wf), (we_h, we), (wd_h, wd), (wb_h, wb), (wu_h, wu), (cot_h, cot), (wj_h, wj))
    ):
        copy = pltpu.make_async_copy(src, dst, load_sem.at[i])
        copy.start()
        loads.append(copy)
    l_vol, l_wf, l_we, l_wd, l_wb, l_wu, l_cot, l_wj = loads

    around = {d: (sec, (me + 16 + d) % 16) for d in (-3, -2, -1, 1, 2, 3)}
    after, before = around[1], around[-1]
    other_core = (sec + 1 - 2 * core, me)
    y_peers = [(sec, my_z * 4 + (my_y + d) % 4) for d in (1, 2, 3)]
    z_peers = [(sec, ((my_z + d) % 4) * 4 + my_y) for d in (1, 2, 3)]
    sec_peers = [((sec + d) % 8, me) for d in range(1, 8)]

    barrier = pltpu.get_barrier_semaphore()
    peers = [*around.values(), *y_peers, *z_peers, *sec_peers]
    for dev in peers:
        pl.semaphore_signal(barrier, inc=1, device_id=dev, device_id_type=MESH)

    r, c = iotas((64, 64))
    for k in range(9):
        oy, oz = k // 3 - 1, k % 3 - 1
        shift[k] = one_hot(((c >> 3) == (r >> 3) + oy) & ((c & 7) == (r & 7) + oz))
    r, c = iotas((64, T))
    for j in range(5):
        hit = None
        for half in range(2 if j < 4 else 1):
            oy, oz = (2 * j + half) // 3 - 1, (2 * j + half) % 3 - 1
            v = c - 64 * half
            here = (v >= 0) & (v < 64) & ((v >> 3) == (r >> 3) + oy) & ((v & 7) == (r & 7) + oz)
            hit = here if hit is None else hit | here
        pairs[j] = one_hot(hit)
    r, c = iotas((16, 16))
    for k in range(9):
        oy, oz = k // 3 - 1, k % 3 - 1
        shift_c[k * 16 : (k + 1) * 16, :] = one_hot(((c >> 2) == (r >> 2) + oy) & ((c & 3) == (r & 3) + oz))
    r, c = iotas((T, T))
    perm[...] = one_hot(r == block_row(c))
    perm_t[...] = one_hot(c == block_row(r))
    half_mask[0] = one_hot(c < 64)
    half_mask[1] = one_hot(c >= 64)
    r, c = iotas((256, 256))
    eye[...] = one_hot(r == c)
    diag[...] = jnp.zeros((T, 2048), BF)
    for lo, hi in PADS:
        packed[:, :, lo * T : hi * T] = jnp.zeros((16, 16, (hi - lo) * T), BF)

    not_first = jnp.where(me > 0, 1.0, 0.0)
    not_last = jnp.where(me < 15, 1.0, 0.0)

    sends = []

    def remote(src, dst, send_sem, recv_sem, dev):
        return pltpu.make_async_remote_copy(
            src_ref=src, dst_ref=dst, send_sem=send_sem, recv_sem=recv_sem, device_id=dev, device_id_type=MESH
        )

    def push(index, src, dst, dev):
        copy = remote(src, dst, h_send.at[index], h_recv.at[index], dev)
        copy.start()
        sends.append(copy)
        return copy

    def swap(index, first, last, got):
        return push(index, last, got.at[0], after), push(index + 1, first, got.at[1], before)

    def arrived(pair, got):
        for copy in pair:
            copy.wait_recv()
        lo = (got[0].astype(F32) * not_first).astype(BF)
        hi = (got[1].astype(F32) * not_last).astype(BF)
        return lo, hi

    def inside(x, first, count, layer_rows):
        layer = lax.broadcasted_iota(jnp.int32, x.shape, 0) // layer_rows + first
        return jnp.where((layer >= 0) & (layer < count), x, 0.0).astype(BF)

    def spread(to, layers, row=0, per=2, width=T):
        step = per * 64 // 64
        for n in range(0, len(layers), step):
            group = layers[n : n + step]
            both = jnp.concatenate(group, axis=1)
            for k in range(9):
                moved = mm(shift[k], both).astype(BF)
                for m in range(len(group)):
                    to[row + (n + m) * 64 : row + (n + m + 1) * 64, k * width : (k + 1) * width] = (
                        moved[:, m * width : (m + 1) * width]
                    )

    def spread_narrow(to, layers, row):
        for n in range(0, len(layers), 2):
            both = jnp.concatenate(
                [jnp.concatenate([x * half_mask[0, 0:64], x * half_mask[1, 0:64]], axis=0) for x in layers[n : n + 2]],
                axis=1,
            )
            for j in range(5):
                moved = mm(pairs[j], both).astype(BF)
                for m in range(2):
                    to[row + (n + m) * 64 : row + (n + m + 1) * 64, j * T : (j + 1) * T] = moved[:, m * T : (m + 1) * T]

    def layers_of(x):
        return [x[i : i + 64] for i in range(0, x.shape[0], 64)]

    def spread_coarse(to, layers):
        moved = mm(shift_c[...], jnp.concatenate(layers, axis=1)).astype(BF)
        for n in range(len(layers)):
            for k in range(9):
                to[n * 16 : (n + 1) * 16, k * 256 : (k + 1) * 256] = (
                    moved[k * 16 : (k + 1) * 16, n * 256 : (n + 1) * 256]
                )

    def conv(b, w, count, rows):
        depth = b.shape[1]
        total = mm(b[0:count], w[0:depth, :])
        for ox in (1, 2):
            total = total + mm(b[ox * rows : ox * rows + count], w[ox * depth : (ox + 1) * depth, :])
        return total

    def conv_back(b, w, count, rows):
        cols = b.shape[1] // 9
        depth = w.shape[0] // 27
        total = jnp.zeros((count, depth), F32)
        for ox in range(3):
            for k in range(9):
                tap = ox * 9 + k
                total = total + mm_t(
                    b[(2 - ox) * rows : (2 - ox) * rows + count, (8 - k) * cols : (9 - k) * cols],
                    w[tap * depth : (tap + 1) * depth, :],
                )
        return total

    def stacked(flat):
        return jnp.concatenate([flat[:, t * T : (t + 1) * T] for t in range(8)], axis=0)

    def grad_128(step_t, part, tiles, half, chunk, tile, begin=0, end=None):
        width = chunk * T

        def piece(n):
            if n >= tiles:
                return jnp.zeros((16, 8, width), F32)
            return mm(step_t, part(n)).reshape(16, 8, width)

        for n in range(begin, end or half, chunk):
            at = (tile + n) * T
            packed[:, :, at : at + width] = jnp.concatenate([piece(n), piece(half + n)], axis=1).astype(BF)

    def grad_256(step_t, part, begin, end, tile):
        for n in range(begin, end, 2):
            at = (tile + n) * T
            packed[:, :, at : at + 256] = mm(step_t, part(n)).reshape(16, 16, 256).astype(BF)

    def turned(x):
        return mm_t(eye[0 : x.shape[1], 0 : x.shape[1]], x).astype(BF)

    def window(b, at, rows, count, chunk):
        per = b.shape[1] // T

        def part(n):
            ox, k = n // per, n % per
            begin = at + ox * rows
            return b[begin : begin + count, k * T : (k + chunk) * T]

        return part

    step_1, step_2 = 1 + 3 * core, 4 - 3 * core
    at_1 = my_y + core * (my_z - my_y)
    at_2 = my_z + core * (my_y - my_z)
    crossing, gathering = {}, {}

    def cross(g):
        first, n = GROUPS[g]
        w = n // 2 * T
        copy = remote(
            packed.at[:, :, ds(first * T + (1 - core) * w, w)],
            r0.at[:, :, pl.ds(first // 2 * T, w)],
            s0.at[g], q0.at[g], other_core,
        )
        copy.start()
        crossing[g] = copy
        sends.append(copy)

    def flow(f):
        g, kind, lo, tiles, how = FLOWS[f]
        refs = flows[f]
        first, n = GROUPS[g]
        e, w = n // 8, tiles * T
        coords = (at_1, at_2, my_x) if kind == "A" else (my_x, at_1, at_2)
        names = "12x" if kind == "A" else "x12"

        def dev(axis, v):
            if names[axis] == "1":
                return (sec, v * step_1 + at_2 * step_2)
            if names[axis] == "2":
                return (sec, at_1 * step_1 + v * step_2)
            return (v * 2 + core, me)

        def go(src, dst, sem, to):
            copy = remote(src, dst, refs["send"].at[sem], refs["recv"].at[sem], to)
            copy.start()
            sends.append(copy)
            return copy

        u = refs["u"][0]

        def build(i, carry):
            for j in range(4):
                p = i * step_1 + j * step_2
                for x in range(4):
                    at = (x * e + lo) * T
                    there = first // 2 * T + at
                    both = packed[p, :, ds(first * T + core * (n // 2 * T) + at, w)] + r0[p, :, there : there + w]
                    if kind == "A":
                        u[i, j * 4 + x] = both
                    else:
                        u[x, i * 4 + j] = both
            return carry

        lax.fori_loop(0, 4, build, 0)
        for axis in range(3):
            m_count = (16, 4, 1)[axis]
            c, u, r = coords[axis], refs["u"][axis], refs["r"][axis]
            sem = axis * 6

            def put(m, value):
                if axis < 2:
                    q = m_count // 4
                    refs["u"][axis + 1][m // q, m % q] = value
                else:
                    own[:, (first // 8 + lo) * T : (first // 8 + lo) * T + w] = value

            if how[axis] == "d":
                copies = [
                    go(u.at[(c + d) % 4], r.at[d - 1], sem + d - 1, dev(axis, (c + d) % 4)) for d in (1, 2, 3)
                ]
                yield
                for copy in copies:
                    copy.wait_recv()
                for m in range(m_count):
                    total = u[c, m].astype(F32)
                    for d in range(3):
                        total = total + r[d, m].astype(F32)
                    put(m, total.astype(BF))
                continue
            c1, c2, c3 = c + 1 - 2 * (c % 2), (c + 2) % 4, 3 - c
            h = m_count // 2
            low, high = pl.ds(0, h), pl.ds(h, h)
            keep, passed, got = refs["keep"][axis], refs["pass"][axis], refs["got"][axis]
            copies = [
                go(u.at[c1, low], r.at[0, low], sem, dev(axis, c1)),
                go(u.at[c3, high], r.at[0, high], sem + 1, dev(axis, c3)),
                go(u.at[c2, low], r.at[1, low], sem + 2, dev(axis, c1)),
                go(u.at[c2, high], r.at[1, high], sem + 3, dev(axis, c3)),
            ]
            yield
            for copy in copies:
                copy.wait_recv()
            for m in range(m_count):
                passed[m] = u[c3 if m < h else c1, m] + r[1, m]
            copies = [
                go(passed.at[low], got.at[low], sem + 4, dev(axis, c3)),
                go(passed.at[high], got.at[high], sem + 5, dev(axis, c1)),
            ]
            for m in range(m_count):
                keep[m] = u[c, m] + r[0, m]
            yield
            for copy in copies:
                copy.wait_recv()
            for m in range(m_count):
                put(m, keep[m] + got[m])

    running, finished = {}, set()

    def go_on(*which):
        for f in which:
            if f not in running:
                g = FLOWS[f][0]
                if g in crossing:
                    crossing.pop(g).wait_recv()
                running[f] = flow(f)
            if next(running[f], True):
                finished.add(f)

    def gather(g, everyone=False):
        first, n = GROUPS[g]
        q, at = n // 8 * T, first // 8 * T
        assert all(f in finished for f in range(len(FLOWS)) if FLOWS[f][0] == g)

        def copy_of(d, source):
            to = (sec + d) % 8 if everyone else (sec + 2 * d) % 8
            return remote(
                own.at[:, pl.ds(at, q)], full.at[:, ds(place_of(source), q)],
                s4.at[g, d - 1], q4.at[g, d - 1], (to, me),
            )

        def place_of(source):
            return first * T + source % 2 * (n // 2 * T) + source // 2 * q

        gathering[g] = []
        for d in range(1, 8) if everyone else (1, 2, 3):
            copy = copy_of(d, sec)
            copy.start()
            sends.append(copy)
            gathering[g].append(copy_of(d, (sec + 8 - (d if everyone else 2 * d)) % 8))
        full[:, ds(place_of(sec), q)] = own[:, at : at + q]

    def share(g):
        first, n = GROUPS[g]
        w = n // 2 * T
        for copy in gathering[g]:
            copy.wait_recv()

        def copy_of(c):
            where = full.at[:, ds(first * T + c * w, w)]
            return remote(where, where, s4.at[g, 7], q4.at[g, 7], other_core)

        copy = copy_of(core)
        copy.start()
        sends.append(copy)
        gathering[g] = [copy_of(1 - core)]

    l_vol.wait()
    l_cot.wait()
    pl.semaphore_wait(barrier, len(peers))
    pushed = {}
    for n, d in enumerate((1, -1, 2, -2, 3, -3)):
        pushed[-d] = push(n, vol, h_vol.at[3 - d], around[d])
    cot_pair = swap(6, cot.at[pl.ds(0, 64)], cot.at[pl.ds(64, 64)], h_cot)
    r, c = iotas((64, T))
    twice = one_hot(r == (c & 63))
    l_wf.wait()
    zero = jnp.zeros((64, T), BF)
    for ox in range(3):
        wx[ox * 640 : ox * 640 + 576, :] = wf[ox * 576 : (ox + 1) * 576, :]
        wx[ox * 640 + 576 : (ox + 1) * 640, :] = zero
    own_layers = layers_of(mm(vol[...], twice).astype(BF))
    spread_narrow(b_v, own_layers, 6 * 64)
    for d in (-1, 1, -2, 2, -3, 3):
        pushed[d].wait_recv()
        got = inside(mm(h_vol[3 + d], twice), 2 * (me + d), 32, 64)
        spread_narrow(b_v, layers_of(got), (3 + d) * T)
    z1_all = conv(b_v, wx, 768, 64)
    z1[...] = z1_all[320:448]
    h1[...] = inside(silu(z1_all), 2 * me - 5, 32, 64)
    spread(b_1, layers_of(h1))
    l_we.wait()
    z2_all = conv(b_1, we, 640, 64)
    z2[...] = z2_all[256:384]
    sk[...] = inside(silu(z2_all), 2 * me - 4, 32, 64)
    for n in range(5):
        moved = mm(perm[...], sk[n * T : (n + 1) * T]).astype(BF)
        for t in range(8):
            blocks[n * 16 : (n + 1) * 16, t * T : (t + 1) * T] = moved[t * 16 : (t + 1) * 16]
    l_wd.wait()
    z3 = mm(blocks[...], wd[...])
    g1 = silu(z3).astype(BF)
    spread_coarse(b_c, [g1[n * 16 : (n + 1) * 16] for n in range(5)])
    l_wb.wait()
    z4 = conv(b_c, wb, 48, 16)
    g2 = inside(silu(z4), me - 1, 16, 16)
    l_wu.wait()
    lifted = mm(g2, wu[...]).astype(BF)
    for n in range(3):
        li[n * T : (n + 1) * T] = mm(perm_t[...], stacked(lifted[n * 16 : (n + 1) * 16])).astype(BF)
    layers = [
        jnp.concatenate([li[n * 64 : (n + 1) * 64], sk[(n + 2) * 64 : (n + 3) * 64]], axis=1) for n in range(6)
    ]
    spread(b_j, layers, 0, 1, 256)
    l_wj.wait()
    z7 = conv(b_j, wj, 256, 64)
    dec_o[...] = silu(z7[64:192]).astype(BF)

    lo, hi = arrived(cot_pair, h_cot)
    cots = jnp.concatenate([lo, cot[...], hi], axis=0)
    t7[...] = (cots.astype(F32) * slope(z7)).astype(BF)
    spread(b_s, layers_of(t7))
    back = conv_back(b_s, wj, T, 64)
    e_skip[...] = back[:, T:256]
    moved = mm(perm[...], back[:, 0:T].astype(BF)).astype(BF)
    lift_blocks = jnp.concatenate([moved[t * 16 : (t + 1) * 16] for t in range(8)], axis=1)
    e3 = mm_t(lift_blocks, wu[...]).astype(BF)
    t4[...] = (e3.astype(F32) * slope(z4[16:32])).astype(BF)
    pair = swap(8, t4, t4, h_t4)
    for t in range(8):
        diag[t * 16 : (t + 1) * 16, t * 256 : (t + 1) * 256] = g2[16:32]
    moved_t = turned(moved)
    for t in range(8):
        up = mm(moved_t, diag[:, t * 256 : (t + 1) * 256]).astype(BF)
        for b in range(8):
            at = UP_AT * T + (b % 4) * 256
            packed[2 * t + b // 4, :, at : at + 256] = up[b * 16 : (b + 1) * 16]
    step_t = turned(t4[...])
    grad_256(step_t, window(b_c, 16, 16, 16, 2), 0, 8, BOTTOM_AT)
    cross(0)
    grad_256(step_t, window(b_c, 16, 16, 16, 2), 8, 24, BOTTOM_AT)
    cross(1)
    grad_256(step_t, window(b_c, 16, 16, 16, 2), 24, 40, BOTTOM_AT)
    cross(2)
    grad_256(step_t, window(b_c, 16, 16, 16, 2), 40, 54, BOTTOM_AT)
    step_t = turned(t7[64:192])
    grad_128(step_t, window(b_j, 64, 64, T, 3), 54, 27, 3, JOIN_AT, 0, 3)
    cross(3)
    grad_128(step_t, window(b_j, 64, 64, T, 3), 54, 27, 3, JOIN_AT, 3, 27)
    cross(4)
    go_on(0)
    before_own = inside(mm(h_vol[2], twice), 2 * (me - 1), 32, 64)
    after_own = inside(mm(h_vol[4], twice), 2 * (me + 1), 32, 64)
    spread(b_d, [before_own[64:128], *layers_of(mm(vol[...], twice).astype(BF)), after_own[0:64]])
    lo, hi = arrived(pair, h_t4)
    spread_coarse(b_4, [lo, t4[...], hi])
    e4 = conv_back(b_4, wb, 16, 16).astype(BF)
    t3 = (e4.astype(F32) * slope(z3[32:48])).astype(BF)
    e5 = stacked(mm_t(t3, wd[...]))
    high = e5.astype(BF)
    low = (e5 - high.astype(F32)).astype(BF)
    e5 = mm(perm_t[...], high) + mm(perm_t[...], low)
    t2[...] = ((e5 + e_skip[...]) * slope(z2[...])).astype(BF)
    pair = swap(10, t2.at[pl.ds(0, 64)], t2.at[pl.ds(64, 64)], h_t2)
    go_on(1, 3, 2, 4)
    grad_256(turned(t3), lambda n: blocks[32:48, n * T : (n + 2) * T], 0, 8, DOWN_AT)
    grad_128(turned(t2[...]), window(b_1, 256, 64, T, 1), 27, 14, 1, ENC_AT)
    cross(5)
    go_on(5, 6, 0)
    spread(b_s, layers_of(t2), 64)
    lo, hi = arrived(pair, h_t2)
    spread(b_s, [lo], 0)
    spread(b_s, [hi], 192)
    back = conv_back(b_s, we, T, 64)
    t1 = (back.astype(BF).astype(F32) * slope(z1[...])).astype(BF)
    for j in range(14):
        left, right = (b_d[t // 9 * 64 : 128 + t // 9 * 64, t % 9 * T : (t % 9 + 1) * T] for t in (2 * j, min(2 * j + 1, 26)))
        tile = left * half_mask[0]
        if j < 13:
            tile = tile + right * half_mask[1]
        a_f[:, j * T : (j + 1) * T] = tile
    grad_128(turned(t1), lambda n: a_f[:, n * T : (n + 1) * T], 14, 7, 1, FIRST_AT)
    cross(6)
    go_on(1, 7, 3, 8, 2, 4, 9, 5, 0, 6, 1, 3, 7, 8, 2, 4, 9, 5, 0, 6, 1, 3, 7, 8, 2, 4, 9, 5, 0, 6, 1, 3, 2, 7, 4)
    gather(3)
    go_on(8)
    gather(2)
    go_on(9, 5, 0)
    gather(0)
    go_on(6)
    gather(4)
    go_on(1)
    gather(1)
    go_on(7, 8)
    gather(5, True)
    share(2)
    go_on(9)
    gather(6, True)
    share(3)
    share(0)
    share(1)
    share(4)
    for g in (0, 1, 2, 3, 4, 5, 6):
        first, n = GROUPS[g]
        for copy in gathering[g]:
            copy.wait_recv()
        full_o[:, first * T : (first + n) * T] = full[:, first * T : (first + n) * T]
    for copy in sends:
        copy.wait_send()


def finish(dec, full, dec_o, gf_o, ge_o, gd_o, gb_o, gu_o, gj_o):
    factor = 1.0 / math.sqrt(16384)
    dec_o[...] = dec[...]

    def rows(tile, width):
        return full[:, tile * T : tile * T + width].astype(F32) * factor

    both = rows(JOIN_AT, 3456)
    gj_o[:, 0:3456] = both[0:8]
    gj_o[:, 3456:6912] = both[8:16]
    for b in range(4):
        gu_o[b * 16 : (b + 1) * 16, :] = rows(UP_AT + 2 * b, 256)
    gb_o[...] = rows(BOTTOM_AT, 6912)
    gd_o[...] = rows(DOWN_AT, 1024)
    both = rows(ENC_AT, 1792)
    ge_o[:, 0:1792] = both[0:8]
    ge_o[:, 1792:3456] = both[8:16, 0:1664]
    both = rows(FIRST_AT, 896)
    gf_o[:, 0:896] = both[0:8]
    gf_o[:, 896:1728] = both[8:16, 0:832]


def flow_scratch(tiles, how):
    v, w = lambda *shape: pltpu.VMEM((*shape, 16, tiles * T), BF), (16, 4, 1)
    two = [how[i] == "b" for i in range(3)]
    return {
        "u": [v(4, m) for m in w],
        "r": [v(2 if two[i] else 3, m) for i, m in enumerate(w)],
        **{name: [v(m) if two[i] else v(1) for i, m in enumerate(w)] for name in ("keep", "pass", "got")},
        "send": pltpu.SemaphoreType.DMA((18,)),
        "recv": pltpu.SemaphoreType.DMA((18,)),
    }


def scratch():
    v, dma = pltpu.VMEM, pltpu.SemaphoreType.DMA
    return [
        v((128, 64), BF), v((1728, 128), BF), v((3456, 128), BF), v((1024, 256), BF), v((6912, 256), BF),
        v((256, 1024), BF), v((6912, 128), BF), v((128, 128), BF), dma((8,)),
        v((9, 64, 64), BF), v((144, 16), BF), v((T, T), BF), v((T, T), BF), v((256, 256), BF), v((2, T, T), BF),
        v((5, 64, T), BF), v((256, 1152), BF), v((1920, T), BF), v((896, 640), BF), v((768, 1152), BF), v((384, 2304), BF), v((256, 1152), BF),
        v((80, 2304), BF), v((48, 2304), BF), v((T, 1792), BF), v((80, 1024), BF), v((T, 2048), BF),
        v((T, T), F32), v((T, T), F32), v((T, T), F32),
        v((768, T), BF), v((640, T), BF), v((384, T), BF), v((256, T), BF), v((T, T), BF), v((16, 256), BF),
        v((7, T, 64), BF), v((2, 64, T), BF), v((2, 64, T), BF), v((2, 16, 256), BF), dma((12,)), dma((12,)),
        v((16, 16, COLS), BF), v((16, 16, HALF), BF), v((16, EIGHTH), BF), v((16, COLS), BF),
        dma((8,)), dma((8,)), dma((8, 8)), dma((8, 8)), [flow_scratch(*f[3:]) for f in FLOWS],
    ]


def body(volume, w_first, w_enc, w_down, w_bottom, w_up, w_join, cotangent):
    out = lambda shape, dtype=F32: jax.ShapeDtypeStruct(shape, dtype)
    done = pl.pallas_call(
        kernel,
        out_shape=(out((128, 128), BF), out((16, COLS), BF)),
        in_specs=[pl.BlockSpec(memory_space=pl.ANY)] * 8,
        out_specs=[pl.BlockSpec(memory_space=pltpu.VMEM)] * 2,
        scratch_shapes=scratch(),
        compiler_params=pltpu.CompilerParams(
            collective_id=0, has_side_effects=True, vmem_limit_bytes=58 * 1024 * 1024
        ),
        name="step",
    )(
        volume.reshape(128, 64), w_first, w_enc, w_down, w_bottom, w_up, w_join, cotangent.reshape(128, 128)
    )
    results = pl.pallas_call(
        finish,
        out_shape=(
            out((128, 128), BF), out((8, 1728)), out((8, 3456)), out((16, 1024)), out((16, 6912)), out((64, 256)),
            out((8, 6912)),
        ),
        name="finish",
    )(*done)
    decoded, *grads = results
    return (decoded.reshape(1, 2, 8, 8, 128), *(g.T for g in grads))


def solution(mesh):
    crops = P("section", "space", None, None, None)
    return jax.shard_map(
        body,
        mesh=mesh,
        in_specs=(crops, P(), P(), P(), P(), P(), P(), crops),
        out_specs=(crops, *([P(None, "space")] * 6)),
        check_vma=False,
    )
```

```python
import math

import jax
import jax.numpy as jnp
from jax import lax
from jax.experimental import pallas as pl
from jax.experimental.pallas import tpu as pltpu
from jax.sharding import PartitionSpec as P

BF = jnp.bfloat16
F32 = jnp.float32
MESH = pl.DeviceIdType.MESH
T = 128
GROUPS = ((0, 16), (16, 16), (32, 16), (48, 16), (64, 24), (88, 24), (112, 8))
UP_AT, BOTTOM_AT, JOIN_AT, DOWN_AT, ENC_AT, FIRST_AT = 0, 8, 62, 89, 97, 112
PADS = ((111, 112), (119, 120))
COLS = 120 * T
HALF, EIGHTH = COLS // 2, COLS // 8
FLOWS = (
    (0, "A", 0, 2, "bbd"),
    (1, "A", 0, 2, "bdd"),
    (2, "X", 0, 2, "bdd"),
    (3, "A", 0, 1, "bdd"),
    (3, "X", 1, 1, "bdd"),
    (4, "A", 0, 3, "bdd"),
    (5, "A", 0, 2, "bdd"),
    (5, "X", 2, 1, "bdd"),
    (6, "X", 0, 1, "bdd"),
)


def mm(a, b):
    return jnp.dot(a, b, preferred_element_type=F32)


def mm_t(a, b):
    return lax.dot_general(a, b, (((1,), (1,)), ((), ())), preferred_element_type=F32)


def silu(z):
    return z * jax.nn.sigmoid(z)


def slope(z):
    s = jax.nn.sigmoid(z)
    return s * (1.0 + z * (1.0 - s))


def one_hot(cond):
    return jnp.where(cond, 1.0, 0.0).astype(BF)


def iotas(shape):
    return lax.broadcasted_iota(jnp.int32, shape, 0), lax.broadcasted_iota(jnp.int32, shape, 1)


def block_row(v):
    y, z = (v >> 3) & 7, v & 7
    return ((v >> 6) * 4 + (y & 1) * 2 + (z & 1)) * 16 + (y >> 1) * 4 + (z >> 1)


def ds(at, size):
    return pl.ds(pl.multiple_of(at, T), size)


def kernel(
    vol_h, wf_h, we_h, wd_h, wb_h, wu_h, wj_h, cot_h,
    dec_o, full_o,
    vol, wf, we, wd, wb, wu, wj, cot, load_sem,
    shift, shift_c, perm, perm_t, eye, half_mask,
    pairs, b_d, wx, b_v, b_1, b_j, b_s, b_c, b_4, a_f, blocks, diag,
    z1, z2, e_skip,
    h1, sk, li, t7, t2, t4,
    h_vol, h_cot, h_t2, h_t4, h_send, h_recv,
    packed, r0, own, full,
    s0, q0, s4, q4, flows,
):
    sec, me = lax.axis_index("section"), lax.axis_index("space")
    core, my_x = sec % 2, sec // 2
    my_z, my_y = me // 4, me % 4

    loads = []
    for i, (src, dst) in enumerate(
        ((vol_h, vol), (wf_h, wf), (we_h, we), (wd_h, wd), (wb_h, wb), (wu_h, wu), (cot_h, cot), (wj_h, wj))
    ):
        copy = pltpu.make_async_copy(src, dst, load_sem.at[i])
        copy.start()
        loads.append(copy)
    l_vol, l_wf, l_we, l_wd, l_wb, l_wu, l_cot, l_wj = loads

    around = {d: (sec, (me + 16 + d) % 16) for d in (-3, -2, -1, 1, 2, 3)}
    after, before = around[1], around[-1]
    other_core = (sec + 1 - 2 * core, me)
    y_peers = [(sec, my_z * 4 + (my_y + d) % 4) for d in (1, 2, 3)]
    z_peers = [(sec, ((my_z + d) % 4) * 4 + my_y) for d in (1, 2, 3)]
    sec_peers = [((sec + d) % 8, me) for d in range(1, 8)]

    barrier = pltpu.get_barrier_semaphore()
    peers = [*around.values(), *y_peers, *z_peers, *sec_peers]
    for dev in peers:
        pl.semaphore_signal(barrier, inc=1, device_id=dev, device_id_type=MESH)

    r, c = iotas((64, 64))
    for k in range(9):
        oy, oz = k // 3 - 1, k % 3 - 1
        shift[k] = one_hot(((c >> 3) == (r >> 3) + oy) & ((c & 7) == (r & 7) + oz))
    r, c = iotas((64, T))
    for j in range(5):
        hit = None
        for half in range(2 if j < 4 else 1):
            oy, oz = (2 * j + half) // 3 - 1, (2 * j + half) % 3 - 1
            v = c - 64 * half
            here = (v >= 0) & (v < 64) & ((v >> 3) == (r >> 3) + oy) & ((v & 7) == (r & 7) + oz)
            hit = here if hit is None else hit | here
        pairs[j] = one_hot(hit)
    r, c = iotas((16, 16))
    for k in range(9):
        oy, oz = k // 3 - 1, k % 3 - 1
        shift_c[k * 16 : (k + 1) * 16, :] = one_hot(((c >> 2) == (r >> 2) + oy) & ((c & 3) == (r & 3) + oz))
    r, c = iotas((T, T))
    perm[...] = one_hot(r == block_row(c))
    perm_t[...] = one_hot(c == block_row(r))
    half_mask[0] = one_hot(c < 64)
    half_mask[1] = one_hot(c >= 64)
    r, c = iotas((256, 256))
    eye[...] = one_hot(r == c)
    diag[...] = jnp.zeros((T, 2048), BF)
    for lo, hi in PADS:
        packed[:, :, lo * T : hi * T] = jnp.zeros((16, 16, (hi - lo) * T), BF)

    not_first = jnp.where(me > 0, 1.0, 0.0)
    not_last = jnp.where(me < 15, 1.0, 0.0)

    sends = []

    def remote(src, dst, send_sem, recv_sem, dev):
        return pltpu.make_async_remote_copy(
            src_ref=src, dst_ref=dst, send_sem=send_sem, recv_sem=recv_sem, device_id=dev, device_id_type=MESH
        )

    def push(index, src, dst, dev):
        copy = remote(src, dst, h_send.at[index], h_recv.at[index], dev)
        copy.start()
        sends.append(copy)
        return copy

    def swap(index, first, last, got):
        return push(index, last, got.at[0], after), push(index + 1, first, got.at[1], before)

    def arrived(pair, got):
        for copy in pair:
            copy.wait_recv()
        lo = (got[0].astype(F32) * not_first).astype(BF)
        hi = (got[1].astype(F32) * not_last).astype(BF)
        return lo, hi

    def inside(x, first, count, layer_rows):
        layer = lax.broadcasted_iota(jnp.int32, x.shape, 0) // layer_rows + first
        return jnp.where((layer >= 0) & (layer < count), x, 0.0).astype(BF)

    def spread(to, layers, row=0, per=2, width=T):
        step = per * 64 // 64
        for n in range(0, len(layers), step):
            group = layers[n : n + step]
            both = jnp.concatenate(group, axis=1)
            for k in range(9):
                moved = mm(shift[k], both).astype(BF)
                for m in range(len(group)):
                    to[row + (n + m) * 64 : row + (n + m + 1) * 64, k * width : (k + 1) * width] = (
                        moved[:, m * width : (m + 1) * width]
                    )

    def spread_narrow(to, layers, row):
        for n in range(0, len(layers), 2):
            both = jnp.concatenate(
                [jnp.concatenate([x * half_mask[0, 0:64], x * half_mask[1, 0:64]], axis=0) for x in layers[n : n + 2]],
                axis=1,
            )
            for j in range(5):
                moved = mm(pairs[j], both).astype(BF)
                for m in range(2):
                    to[row + (n + m) * 64 : row + (n + m + 1) * 64, j * T : (j + 1) * T] = moved[:, m * T : (m + 1) * T]

    def layers_of(x):
        return [x[i : i + 64] for i in range(0, x.shape[0], 64)]

    def spread_coarse(to, layers):
        moved = mm(shift_c[...], jnp.concatenate(layers, axis=1)).astype(BF)
        for n in range(len(layers)):
            for k in range(9):
                to[n * 16 : (n + 1) * 16, k * 256 : (k + 1) * 256] = (
                    moved[k * 16 : (k + 1) * 16, n * 256 : (n + 1) * 256]
                )

    def conv(b, w, count, rows):
        depth = b.shape[1]
        total = mm(b[0:count], w[0:depth, :])
        for ox in (1, 2):
            total = total + mm(b[ox * rows : ox * rows + count], w[ox * depth : (ox + 1) * depth, :])
        return total

    def conv_back(b, w, count, rows):
        cols = b.shape[1] // 9
        depth = w.shape[0] // 27
        total = jnp.zeros((count, depth), F32)
        for ox in range(3):
            for k in range(9):
                tap = ox * 9 + k
                total = total + mm_t(
                    b[(2 - ox) * rows : (2 - ox) * rows + count, (8 - k) * cols : (9 - k) * cols],
                    w[tap * depth : (tap + 1) * depth, :],
                )
        return total

    def stacked(flat):
        return jnp.concatenate([flat[:, t * T : (t + 1) * T] for t in range(8)], axis=0)

    def grad_128(step_t, part, tiles, half, chunk, tile, begin=0, end=None):
        width = chunk * T

        def piece(n):
            if n >= tiles:
                return jnp.zeros((16, 8, width), F32)
            return mm(step_t, part(n)).reshape(16, 8, width)

        for n in range(begin, end or half, chunk):
            at = (tile + n) * T
            packed[:, :, at : at + width] = jnp.concatenate([piece(n), piece(half + n)], axis=1).astype(BF)

    def grad_256(step_t, part, begin, end, tile):
        for n in range(begin, end, 2):
            at = (tile + n) * T
            packed[:, :, at : at + 256] = mm(step_t, part(n)).reshape(16, 16, 256).astype(BF)

    def turned(x):
        return mm_t(eye[0 : x.shape[1], 0 : x.shape[1]], x).astype(BF)

    def window(b, at, rows, count, chunk):
        per = b.shape[1] // T

        def part(n):
            ox, k = n // per, n % per
            begin = at + ox * rows
            return b[begin : begin + count, k * T : (k + chunk) * T]

        return part

    step_1, step_2 = 1 + 3 * core, 4 - 3 * core
    at_1 = my_y + core * (my_z - my_y)
    at_2 = my_z + core * (my_y - my_z)
    crossing, gathering = {}, {}

    def cross(g):
        first, n = GROUPS[g]
        w = n // 2 * T
        copy = remote(
            packed.at[:, :, ds(first * T + (1 - core) * w, w)],
            r0.at[:, :, pl.ds(first // 2 * T, w)],
            s0.at[g], q0.at[g], other_core,
        )
        copy.start()
        crossing[g] = copy
        sends.append(copy)

    def flow(f):
        g, kind, lo, tiles, how = FLOWS[f]
        refs = flows[f]
        first, n = GROUPS[g]
        e, w = n // 8, tiles * T
        coords = (at_1, at_2, my_x) if kind == "A" else (my_x, at_1, at_2)
        names = "12x" if kind == "A" else "x12"

        def dev(axis, v):
            if names[axis] == "1":
                return (sec, v * step_1 + at_2 * step_2)
            if names[axis] == "2":
                return (sec, at_1 * step_1 + v * step_2)
            return (v * 2 + core, me)

        def go(src, dst, sem, to):
            copy = remote(src, dst, refs["send"].at[sem], refs["recv"].at[sem], to)
            copy.start()
            sends.append(copy)
            return copy

        u = refs["u"][0]

        def build(i, carry):
            for j in range(4):
                p = i * step_1 + j * step_2
                for x in range(4):
                    at = (x * e + lo) * T
                    there = first // 2 * T + at
                    both = packed[p, :, ds(first * T + core * (n // 2 * T) + at, w)] + r0[p, :, there : there + w]
                    if kind == "A":
                        u[i, j * 4 + x] = both
                    else:
                        u[x, i * 4 + j] = both
            return carry

        lax.fori_loop(0, 4, build, 0)
        for axis in range(3):
            m_count = (16, 4, 1)[axis]
            c, u, r = coords[axis], refs["u"][axis], refs["r"][axis]
            sem = axis * 6

            def put(m, value):
                if axis < 2:
                    q = m_count // 4
                    refs["u"][axis + 1][m // q, m % q] = value
                else:
                    own[:, (first // 8 + lo) * T : (first // 8 + lo) * T + w] = value

            if how[axis] == "d":
                copies = [
                    go(u.at[(c + d) % 4], r.at[d - 1], sem + d - 1, dev(axis, (c + d) % 4)) for d in (1, 2, 3)
                ]
                yield
                for copy in copies:
                    copy.wait_recv()
                for m in range(m_count):
                    total = u[c, m].astype(F32)
                    for d in range(3):
                        total = total + r[d, m].astype(F32)
                    put(m, total.astype(BF))
                continue
            c1, c2, c3 = c + 1 - 2 * (c % 2), (c + 2) % 4, 3 - c
            h = m_count // 2
            low, high = pl.ds(0, h), pl.ds(h, h)
            keep, passed, got = refs["keep"][axis], refs["pass"][axis], refs["got"][axis]
            copies = [
                go(u.at[c1, low], r.at[0, low], sem, dev(axis, c1)),
                go(u.at[c3, high], r.at[0, high], sem + 1, dev(axis, c3)),
                go(u.at[c2, low], r.at[1, low], sem + 2, dev(axis, c1)),
                go(u.at[c2, high], r.at[1, high], sem + 3, dev(axis, c3)),
            ]
            yield
            for copy in copies:
                copy.wait_recv()
            for m in range(m_count):
                passed[m] = u[c3 if m < h else c1, m] + r[1, m]
            copies = [
                go(passed.at[low], got.at[low], sem + 4, dev(axis, c3)),
                go(passed.at[high], got.at[high], sem + 5, dev(axis, c1)),
            ]
            for m in range(m_count):
                keep[m] = u[c, m] + r[0, m]
            yield
            for copy in copies:
                copy.wait_recv()
            for m in range(m_count):
                put(m, keep[m] + got[m])

    running, finished = {}, set()

    def go_on(*which):
        for f in which:
            if f not in running:
                g = FLOWS[f][0]
                if g in crossing:
                    crossing.pop(g).wait_recv()
                running[f] = flow(f)
            if next(running[f], True):
                finished.add(f)

    def gather(g, everyone=False):
        first, n = GROUPS[g]
        q, at = n // 8 * T, first // 8 * T
        assert all(f in finished for f in range(len(FLOWS)) if FLOWS[f][0] == g)

        def copy_of(d, source):
            to = (sec + d) % 8 if everyone else (sec + 2 * d) % 8
            return remote(
                own.at[:, pl.ds(at, q)], full.at[:, ds(place_of(source), q)],
                s4.at[g, d - 1], q4.at[g, d - 1], (to, me),
            )

        def place_of(source):
            return first * T + source % 2 * (n // 2 * T) + source // 2 * q

        gathering[g] = []
        for d in range(1, 8) if everyone else (1, 2, 3):
            copy = copy_of(d, sec)
            copy.start()
            sends.append(copy)
            gathering[g].append(copy_of(d, (sec + 8 - (d if everyone else 2 * d)) % 8))
        full[:, ds(place_of(sec), q)] = own[:, at : at + q]

    def share(g):
        first, n = GROUPS[g]
        w = n // 2 * T
        for copy in gathering[g]:
            copy.wait_recv()

        def copy_of(c):
            where = full.at[:, ds(first * T + c * w, w)]
            return remote(where, where, s4.at[g, 7], q4.at[g, 7], other_core)

        copy = copy_of(core)
        copy.start()
        sends.append(copy)
        gathering[g] = [copy_of(1 - core)]

    l_vol.wait()
    l_cot.wait()
    pl.semaphore_wait(barrier, len(peers))
    pushed = {}
    for n, d in enumerate((3, -3, 2, -2, 1, -1)):
        pushed[-d] = push(n, vol, h_vol.at[3 - d], around[d])
    cot_pair = swap(6, cot.at[pl.ds(0, 64)], cot.at[pl.ds(64, 64)], h_cot)
    r, c = iotas((64, T))
    twice = one_hot(r == (c & 63))
    l_wf.wait()
    zero = jnp.zeros((64, T), BF)
    for ox in range(3):
        wx[ox * 640 : ox * 640 + 576, :] = wf[ox * 576 : (ox + 1) * 576, :]
        wx[ox * 640 + 576 : (ox + 1) * 640, :] = zero
    own_layers = layers_of(mm(vol[...], twice).astype(BF))
    spread_narrow(b_v, own_layers, 6 * 64)
    spread(b_d, own_layers, 64)
    for d in (-1, 1, -2, 2, -3, 3):
        pushed[d].wait_recv()
        got = inside(mm(h_vol[3 + d], twice), 2 * (me + d), 32, 64)
        spread_narrow(b_v, layers_of(got), (3 + d) * T)
    z1_all = conv(b_v, wx, 768, 64)
    z1[...] = z1_all[320:448]
    h1[...] = inside(silu(z1_all), 2 * me - 5, 32, 64)
    spread(b_1, layers_of(h1))
    l_we.wait()
    z2_all = conv(b_1, we, 640, 64)
    z2[...] = z2_all[256:384]
    sk[...] = inside(silu(z2_all), 2 * me - 4, 32, 64)
    for n in range(5):
        moved = mm(perm[...], sk[n * T : (n + 1) * T]).astype(BF)
        for t in range(8):
            blocks[n * 16 : (n + 1) * 16, t * T : (t + 1) * T] = moved[t * 16 : (t + 1) * 16]
    l_wd.wait()
    z3 = mm(blocks[...], wd[...])
    g1 = silu(z3).astype(BF)
    spread_coarse(b_c, [g1[n * 16 : (n + 1) * 16] for n in range(5)])
    l_wb.wait()
    z4 = conv(b_c, wb, 48, 16)
    g2 = inside(silu(z4), me - 1, 16, 16)
    l_wu.wait()
    lifted = mm(g2, wu[...]).astype(BF)
    for n in range(3):
        li[n * T : (n + 1) * T] = mm(perm_t[...], stacked(lifted[n * 16 : (n + 1) * 16])).astype(BF)
    layers = [
        jnp.concatenate([li[n * 64 : (n + 1) * 64], sk[(n + 2) * 64 : (n + 3) * 64]], axis=1) for n in range(6)
    ]
    spread(b_j, layers, 0, 1, 256)
    l_wj.wait()
    z7 = conv(b_j, wj, 256, 64)
    dec_o[...] = silu(z7[64:192]).astype(BF)

    lo, hi = arrived(cot_pair, h_cot)
    cots = jnp.concatenate([lo, cot[...], hi], axis=0)
    t7[...] = (cots.astype(F32) * slope(z7)).astype(BF)
    spread(b_s, layers_of(t7))
    back = conv_back(b_s, wj, T, 64)
    e_skip[...] = back[:, T:256]
    moved = mm(perm[...], back[:, 0:T].astype(BF)).astype(BF)
    lift_blocks = jnp.concatenate([moved[t * 16 : (t + 1) * 16] for t in range(8)], axis=1)
    e3 = mm_t(lift_blocks, wu[...]).astype(BF)
    t4[...] = (e3.astype(F32) * slope(z4[16:32])).astype(BF)
    pair = swap(8, t4, t4, h_t4)
    for t in range(8):
        diag[t * 16 : (t + 1) * 16, t * 256 : (t + 1) * 256] = g2[16:32]
    moved_t = turned(moved)
    for t in range(8):
        up = mm(moved_t, diag[:, t * 256 : (t + 1) * 256]).astype(BF)
        for b in range(8):
            at = UP_AT * T + (b % 4) * 256
            packed[2 * t + b // 4, :, at : at + 256] = up[b * 16 : (b + 1) * 16]
    step_t = turned(t4[...])
    grad_256(step_t, window(b_c, 16, 16, 16, 2), 0, 8, BOTTOM_AT)
    cross(0)
    grad_256(step_t, window(b_c, 16, 16, 16, 2), 8, 24, BOTTOM_AT)
    cross(1)
    grad_256(step_t, window(b_c, 16, 16, 16, 2), 24, 40, BOTTOM_AT)
    cross(2)
    grad_256(step_t, window(b_c, 16, 16, 16, 2), 40, 54, BOTTOM_AT)
    step_t = turned(t7[64:192])
    grad_128(step_t, window(b_j, 64, 64, T, 3), 54, 27, 3, JOIN_AT, 0, 3)
    cross(3)
    grad_128(step_t, window(b_j, 64, 64, T, 3), 54, 27, 3, JOIN_AT, 3, 27)
    cross(4)
    go_on(0)
    lo, hi = arrived(pair, h_t4)
    spread_coarse(b_4, [lo, t4[...], hi])
    e4 = conv_back(b_4, wb, 16, 16).astype(BF)
    t3 = (e4.astype(F32) * slope(z3[32:48])).astype(BF)
    e5 = stacked(mm_t(t3, wd[...]))
    high = e5.astype(BF)
    low = (e5 - high.astype(F32)).astype(BF)
    e5 = mm(perm_t[...], high) + mm(perm_t[...], low)
    t2[...] = ((e5 + e_skip[...]) * slope(z2[...])).astype(BF)
    pair = swap(10, t2.at[pl.ds(0, 64)], t2.at[pl.ds(64, 64)], h_t2)
    go_on(1, 2, 4, 3)
    grad_256(turned(t3), lambda n: blocks[32:48, n * T : (n + 2) * T], 0, 8, DOWN_AT)
    grad_128(turned(t2[...]), window(b_1, 256, 64, T, 1), 27, 14, 1, ENC_AT)
    cross(5)
    go_on(5)
    spread(b_s, layers_of(t2), 64)
    go_on(0)
    before_own = inside(mm(h_vol[2], twice), 2 * (me - 1), 32, 64)
    after_own = inside(mm(h_vol[4], twice), 2 * (me + 1), 32, 64)
    spread(b_d, [before_own[64:128]], 0)
    spread(b_d, [after_own[0:64]], 192)
    lo, hi = arrived(pair, h_t2)
    spread(b_s, [lo], 0)
    spread(b_s, [hi], 192)
    back = conv_back(b_s, we, T, 64)
    t1 = (back.astype(BF).astype(F32) * slope(z1[...])).astype(BF)
    for j in range(14):
        left, right = (b_d[t // 9 * 64 : 128 + t // 9 * 64, t % 9 * T : (t % 9 + 1) * T] for t in (2 * j, min(2 * j + 1, 26)))
        tile = left * half_mask[0]
        if j < 13:
            tile = tile + right * half_mask[1]
        a_f[:, j * T : (j + 1) * T] = tile
    grad_128(turned(t1), lambda n: a_f[:, n * T : (n + 1) * T], 14, 7, 1, FIRST_AT)
    cross(6)
    go_on(1, 6, 7, 3, 2, 8, 4, 5, 0, 1, 6, 7, 3, 2, 0, 5, 8, 1, 4, 6, 7, 3, 0, 2, 8, 1)
    gather(1)
    go_on(5, 4, 3, 6, 7, 0)
    gather(0)
    go_on(2)
    gather(2)
    go_on(8, 4)
    gather(3)
    share(1)
    go_on(5)
    gather(4)
    go_on(6, 7)
    gather(5, True)
    go_on(8)
    gather(6, True)
    share(2)
    share(3)
    share(0)
    share(4)
    for g in (0, 1, 2, 3, 4, 5, 6):
        first, n = GROUPS[g]
        for copy in gathering[g]:
            copy.wait_recv()
        full_o[:, first * T : (first + n) * T] = full[:, first * T : (first + n) * T]
    for copy in sends:
        copy.wait_send()


def finish(dec, full, dec_o, gf_o, ge_o, gd_o, gb_o, gu_o, gj_o):
    factor = 1.0 / math.sqrt(16384)
    dec_o[...] = dec[...]

    def rows(tile, width):
        return full[:, tile * T : tile * T + width].astype(F32) * factor

    both = rows(JOIN_AT, 3456)
    gj_o[:, 0:3456] = both[0:8]
    gj_o[:, 3456:6912] = both[8:16]
    for b in range(4):
        gu_o[b * 16 : (b + 1) * 16, :] = rows(UP_AT + 2 * b, 256)
    gb_o[...] = rows(BOTTOM_AT, 6912)
    gd_o[...] = rows(DOWN_AT, 1024)
    both = rows(ENC_AT, 1792)
    ge_o[:, 0:1792] = both[0:8]
    ge_o[:, 1792:3456] = both[8:16, 0:1664]
    both = rows(FIRST_AT, 896)
    gf_o[:, 0:896] = both[0:8]
    gf_o[:, 896:1728] = both[8:16, 0:832]


def flow_scratch(tiles, how):
    v, w = lambda *shape: pltpu.VMEM((*shape, 16, tiles * T), BF), (16, 4, 1)
    two = [how[i] == "b" for i in range(3)]
    return {
        "u": [v(4, m) for m in w],
        "r": [v(2 if two[i] else 3, m) for i, m in enumerate(w)],
        **{name: [v(m) if two[i] else v(1) for i, m in enumerate(w)] for name in ("keep", "pass", "got")},
        "send": pltpu.SemaphoreType.DMA((18,)),
        "recv": pltpu.SemaphoreType.DMA((18,)),
    }


def scratch():
    v, dma = pltpu.VMEM, pltpu.SemaphoreType.DMA
    return [
        v((128, 64), BF), v((1728, 128), BF), v((3456, 128), BF), v((1024, 256), BF), v((6912, 256), BF),
        v((256, 1024), BF), v((6912, 128), BF), v((128, 128), BF), dma((8,)),
        v((9, 64, 64), BF), v((144, 16), BF), v((T, T), BF), v((T, T), BF), v((256, 256), BF), v((2, T, T), BF),
        v((5, 64, T), BF), v((256, 1152), BF), v((1920, T), BF), v((896, 640), BF), v((768, 1152), BF), v((384, 2304), BF), v((256, 1152), BF),
        v((80, 2304), BF), v((48, 2304), BF), v((T, 1792), BF), v((80, 1024), BF), v((T, 2048), BF),
        v((T, T), F32), v((T, T), F32), v((T, T), F32),
        v((768, T), BF), v((640, T), BF), v((384, T), BF), v((256, T), BF), v((T, T), BF), v((16, 256), BF),
        v((7, T, 64), BF), v((2, 64, T), BF), v((2, 64, T), BF), v((2, 16, 256), BF), dma((12,)), dma((12,)),
        v((16, 16, COLS), BF), v((16, 16, HALF), BF), v((16, EIGHTH), BF), v((16, COLS), BF),
        dma((8,)), dma((8,)), dma((8, 8)), dma((8, 8)), [flow_scratch(*f[3:]) for f in FLOWS],
    ]


def body(volume, w_first, w_enc, w_down, w_bottom, w_up, w_join, cotangent):
    out = lambda shape, dtype=F32: jax.ShapeDtypeStruct(shape, dtype)
    done = pl.pallas_call(
        kernel,
        out_shape=(out((128, 128), BF), out((16, COLS), BF)),
        in_specs=[pl.BlockSpec(memory_space=pl.ANY)] * 8,
        out_specs=[pl.BlockSpec(memory_space=pltpu.VMEM)] * 2,
        scratch_shapes=scratch(),
        compiler_params=pltpu.CompilerParams(
            collective_id=0, has_side_effects=True, vmem_limit_bytes=58 * 1024 * 1024
        ),
        name="step",
    )(
        volume.reshape(128, 64), w_first, w_enc, w_down, w_bottom, w_up, w_join, cotangent.reshape(128, 128)
    )
    results = pl.pallas_call(
        finish,
        out_shape=(
            out((128, 128), BF), out((8, 1728)), out((8, 3456)), out((16, 1024)), out((16, 6912)), out((64, 256)),
            out((8, 6912)),
        ),
        name="finish",
    )(*done)
    decoded, *grads = results
    return (decoded.reshape(1, 2, 8, 8, 128), *(g.T for g in grads))


def solution(mesh):
    crops = P("section", "space", None, None, None)
    return jax.shard_map(
        body,
        mesh=mesh,
        in_specs=(crops, P(), P(), P(), P(), P(), P(), crops),
        out_specs=(crops, *([P(None, "space")] * 6)),
        check_vma=False,
    )
```

```python
import math

import jax
import jax.numpy as jnp
from jax import lax
from jax.experimental import pallas as pl
from jax.experimental.pallas import tpu as pltpu
from jax.sharding import PartitionSpec as P

BF = jnp.bfloat16
F32 = jnp.float32
MESH = pl.DeviceIdType.MESH
T = 128
GROUPS = ((0, 16), (16, 16), (32, 16), (48, 16), (64, 24), (88, 24), (112, 8))
UP_AT, BOTTOM_AT, JOIN_AT, DOWN_AT, ENC_AT, FIRST_AT = 0, 8, 62, 89, 97, 112
PADS = ((111, 112), (119, 120))
COLS = 120 * T
HALF, EIGHTH = COLS // 2, COLS // 8
FLOWS = (
    (0, "A", 0, 2, "bbd"),
    (1, "A", 0, 2, "bbd"),
    (2, "A", 0, 1, "bdd"),
    (2, "X", 1, 1, "bdd"),
    (3, "A", 0, 2, "bdd"),
    (4, "A", 0, 1, "bdd"),
    (4, "X", 1, 2, "bdd"),
    (5, "A", 0, 2, "bdd"),
    (5, "X", 2, 1, "bdd"),
    (6, "A", 0, 1, "bdd"),
)


def mm(a, b):
    return jnp.dot(a, b, preferred_element_type=F32)


def mm_t(a, b):
    return lax.dot_general(a, b, (((1,), (1,)), ((), ())), preferred_element_type=F32)


def silu(z):
    return z * jax.nn.sigmoid(z)


def slope(z):
    s = jax.nn.sigmoid(z)
    return s * (1.0 + z * (1.0 - s))


def one_hot(cond):
    return jnp.where(cond, 1.0, 0.0).astype(BF)


def iotas(shape):
    return lax.broadcasted_iota(jnp.int32, shape, 0), lax.broadcasted_iota(jnp.int32, shape, 1)


def block_row(v):
    y, z = (v >> 3) & 7, v & 7
    return ((v >> 6) * 4 + (y & 1) * 2 + (z & 1)) * 16 + (y >> 1) * 4 + (z >> 1)


def ds(at, size):
    return pl.ds(pl.multiple_of(at, T), size)


def kernel(
    vol_h, wf_h, we_h, wd_h, wb_h, wu_h, wj_h, cot_h,
    dec_o, full_o,
    vol, wf, we, wd, wb, wu, wj, cot, load_sem,
    shift, shift_c, perm, perm_t, eye, half_mask,
    pairs, b_d, wx, b_v, b_1, b_j, b_s, b_c, b_4, a_f, blocks, diag,
    z1, z2, e_skip,
    h1, sk, li, t7, t2, t4,
    h_vol, h_cot, h_t2, h_t4, h_send, h_recv,
    packed, r0, own, full,
    s0, q0, s4, q4, flows,
):
    sec, me = lax.axis_index("section"), lax.axis_index("space")
    core, my_x = sec % 2, sec // 2
    my_z, my_y = me // 4, me % 4

    loads = []
    for i, (src, dst) in enumerate(
        ((vol_h, vol), (wf_h, wf), (we_h, we), (wd_h, wd), (wb_h, wb), (wu_h, wu), (cot_h, cot), (wj_h, wj))
    ):
        copy = pltpu.make_async_copy(src, dst, load_sem.at[i])
        copy.start()
        loads.append(copy)
    l_vol, l_wf, l_we, l_wd, l_wb, l_wu, l_cot, l_wj = loads

    around = {d: (sec, (me + 16 + d) % 16) for d in (-3, -2, -1, 1, 2, 3)}
    after, before = around[1], around[-1]
    other_core = (sec + 1 - 2 * core, me)
    y_peers = [(sec, my_z * 4 + (my_y + d) % 4) for d in (1, 2, 3)]
    z_peers = [(sec, ((my_z + d) % 4) * 4 + my_y) for d in (1, 2, 3)]
    sec_peers = [((sec + d) % 8, me) for d in range(1, 8)]

    barrier = pltpu.get_barrier_semaphore()
    peers = [*around.values(), *y_peers, *z_peers, *sec_peers]
    for dev in peers:
        pl.semaphore_signal(barrier, inc=1, device_id=dev, device_id_type=MESH)

    r, c = iotas((64, 64))
    for k in range(9):
        oy, oz = k // 3 - 1, k % 3 - 1
        shift[k] = one_hot(((c >> 3) == (r >> 3) + oy) & ((c & 7) == (r & 7) + oz))
    r, c = iotas((64, T))
    for j in range(5):
        hit = None
        for half in range(2 if j < 4 else 1):
            oy, oz = (2 * j + half) // 3 - 1, (2 * j + half) % 3 - 1
            v = c - 64 * half
            here = (v >= 0) & (v < 64) & ((v >> 3) == (r >> 3) + oy) & ((v & 7) == (r & 7) + oz)
            hit = here if hit is None else hit | here
        pairs[j] = one_hot(hit)
    r, c = iotas((16, 16))
    for k in range(9):
        oy, oz = k // 3 - 1, k % 3 - 1
        shift_c[k * 16 : (k + 1) * 16, :] = one_hot(((c >> 2) == (r >> 2) + oy) & ((c & 3) == (r & 3) + oz))
    r, c = iotas((T, T))
    perm[...] = one_hot(r == block_row(c))
    perm_t[...] = one_hot(c == block_row(r))
    half_mask[0] = one_hot(c < 64)
    half_mask[1] = one_hot(c >= 64)
    r, c = iotas((256, 256))
    eye[...] = one_hot(r == c)
    diag[...] = jnp.zeros((T, 2048), BF)
    for lo, hi in PADS:
        packed[:, :, lo * T : hi * T] = jnp.zeros((16, 16, (hi - lo) * T), BF)

    not_first = jnp.where(me > 0, 1.0, 0.0)
    not_last = jnp.where(me < 15, 1.0, 0.0)

    sends = []

    def remote(src, dst, send_sem, recv_sem, dev):
        return pltpu.make_async_remote_copy(
            src_ref=src, dst_ref=dst, send_sem=send_sem, recv_sem=recv_sem, device_id=dev, device_id_type=MESH
        )

    def push(index, src, dst, dev):
        copy = remote(src, dst, h_send.at[index], h_recv.at[index], dev)
        copy.start()
        sends.append(copy)
        return copy

    def swap(index, first, last, got):
        return push(index, last, got.at[0], after), push(index + 1, first, got.at[1], before)

    def arrived(pair, got):
        for copy in pair:
            copy.wait_recv()
        lo = (got[0].astype(F32) * not_first).astype(BF)
        hi = (got[1].astype(F32) * not_last).astype(BF)
        return lo, hi

    def inside(x, first, count, layer_rows):
        layer = lax.broadcasted_iota(jnp.int32, x.shape, 0) // layer_rows + first
        return jnp.where((layer >= 0) & (layer < count), x, 0.0).astype(BF)

    def spread(to, layers, row=0, per=2, width=T):
        step = per * 64 // 64
        for n in range(0, len(layers), step):
            group = layers[n : n + step]
            both = jnp.concatenate(group, axis=1)
            for k in range(9):
                moved = mm(shift[k], both).astype(BF)
                for m in range(len(group)):
                    to[row + (n + m) * 64 : row + (n + m + 1) * 64, k * width : (k + 1) * width] = (
                        moved[:, m * width : (m + 1) * width]
                    )

    def spread_narrow(to, layers, row):
        for n in range(0, len(layers), 2):
            both = jnp.concatenate(
                [jnp.concatenate([x * half_mask[0, 0:64], x * half_mask[1, 0:64]], axis=0) for x in layers[n : n + 2]],
                axis=1,
            )
            for j in range(5):
                moved = mm(pairs[j], both).astype(BF)
                for m in range(2):
                    to[row + (n + m) * 64 : row + (n + m + 1) * 64, j * T : (j + 1) * T] = moved[:, m * T : (m + 1) * T]

    def layers_of(x):
        return [x[i : i + 64] for i in range(0, x.shape[0], 64)]

    def spread_coarse(to, layers):
        moved = mm(shift_c[...], jnp.concatenate(layers, axis=1)).astype(BF)
        for n in range(len(layers)):
            for k in range(9):
                to[n * 16 : (n + 1) * 16, k * 256 : (k + 1) * 256] = (
                    moved[k * 16 : (k + 1) * 16, n * 256 : (n + 1) * 256]
                )

    def conv(b, w, count, rows):
        depth = b.shape[1]
        total = mm(b[0:count], w[0:depth, :])
        for ox in (1, 2):
            total = total + mm(b[ox * rows : ox * rows + count], w[ox * depth : (ox + 1) * depth, :])
        return total

    def conv_back(b, w, count, rows):
        cols = b.shape[1] // 9
        depth = w.shape[0] // 27
        total = jnp.zeros((count, depth), F32)
        for ox in range(3):
            for k in range(9):
                tap = ox * 9 + k
                total = total + mm_t(
                    b[(2 - ox) * rows : (2 - ox) * rows + count, (8 - k) * cols : (9 - k) * cols],
                    w[tap * depth : (tap + 1) * depth, :],
                )
        return total

    def stacked(flat):
        return jnp.concatenate([flat[:, t * T : (t + 1) * T] for t in range(8)], axis=0)

    def grad_128(step_t, part, tiles, half, chunk, tile, begin=0, end=None):
        width = chunk * T

        def piece(n):
            if n >= tiles:
                return jnp.zeros((16, 8, width), F32)
            return mm(step_t, part(n)).reshape(16, 8, width)

        for n in range(begin, end or half, chunk):
            at = (tile + n) * T
            packed[:, :, at : at + width] = jnp.concatenate([piece(n), piece(half + n)], axis=1).astype(BF)

    def grad_256(step_t, part, begin, end, tile):
        for n in range(begin, end, 2):
            at = (tile + n) * T
            packed[:, :, at : at + 256] = mm(step_t, part(n)).reshape(16, 16, 256).astype(BF)

    def turned(x):
        return mm_t(eye[0 : x.shape[1], 0 : x.shape[1]], x).astype(BF)

    def window(b, at, rows, count, chunk):
        per = b.shape[1] // T

        def part(n):
            ox, k = n // per, n % per
            begin = at + ox * rows
            return b[begin : begin + count, k * T : (k + chunk) * T]

        return part

    step_1, step_2 = 1 + 3 * core, 4 - 3 * core
    at_1 = my_y + core * (my_z - my_y)
    at_2 = my_z + core * (my_y - my_z)
    crossing, gathering = {}, {}

    def cross(g):
        first, n = GROUPS[g]
        w = n // 2 * T
        copy = remote(
            packed.at[:, :, ds(first * T + (1 - core) * w, w)],
            r0.at[:, :, pl.ds(first // 2 * T, w)],
            s0.at[g], q0.at[g], other_core,
        )
        copy.start()
        crossing[g] = copy
        sends.append(copy)

    def flow(f):
        g, kind, lo, tiles, how = FLOWS[f]
        refs = flows[f]
        first, n = GROUPS[g]
        e, w = n // 8, tiles * T
        coords = (at_1, at_2, my_x) if kind == "A" else (my_x, at_1, at_2)
        names = "12x" if kind == "A" else "x12"

        def dev(axis, v):
            if names[axis] == "1":
                return (sec, v * step_1 + at_2 * step_2)
            if names[axis] == "2":
                return (sec, at_1 * step_1 + v * step_2)
            return (v * 2 + core, me)

        def go(src, dst, sem, to):
            copy = remote(src, dst, refs["send"].at[sem], refs["recv"].at[sem], to)
            copy.start()
            sends.append(copy)
            return copy

        u = refs["u"][0]

        def build(i, carry):
            for j in range(4):
                p = i * step_1 + j * step_2
                for x in range(4):
                    at = (x * e + lo) * T
                    there = first // 2 * T + at
                    both = packed[p, :, ds(first * T + core * (n // 2 * T) + at, w)] + r0[p, :, there : there + w]
                    if kind == "A":
                        u[i, j * 4 + x] = both
                    else:
                        u[x, i * 4 + j] = both
            return carry

        lax.fori_loop(0, 4, build, 0)
        for axis in range(3):
            m_count = (16, 4, 1)[axis]
            c, u, r = coords[axis], refs["u"][axis], refs["r"][axis]
            sem = axis * 6

            def put(m, value):
                if axis < 2:
                    q = m_count // 4
                    refs["u"][axis + 1][m // q, m % q] = value
                else:
                    own[:, (first // 8 + lo) * T : (first // 8 + lo) * T + w] = value

            if how[axis] == "d":
                copies = [
                    go(u.at[(c + d) % 4], r.at[d - 1], sem + d - 1, dev(axis, (c + d) % 4)) for d in (1, 2, 3)
                ]
                yield
                for copy in copies:
                    copy.wait_recv()
                for m in range(m_count):
                    total = u[c, m].astype(F32)
                    for d in range(3):
                        total = total + r[d, m].astype(F32)
                    put(m, total.astype(BF))
                continue
            c1, c2, c3 = c + 1 - 2 * (c % 2), (c + 2) % 4, 3 - c
            h = m_count // 2
            low, high = pl.ds(0, h), pl.ds(h, h)
            keep, passed, got = refs["keep"][axis], refs["pass"][axis], refs["got"][axis]
            copies = [
                go(u.at[c1, low], r.at[0, low], sem, dev(axis, c1)),
                go(u.at[c3, high], r.at[0, high], sem + 1, dev(axis, c3)),
                go(u.at[c2, low], r.at[1, low], sem + 2, dev(axis, c1)),
                go(u.at[c2, high], r.at[1, high], sem + 3, dev(axis, c3)),
            ]
            yield
            for copy in copies:
                copy.wait_recv()
            for m in range(m_count):
                passed[m] = u[c3 if m < h else c1, m] + r[1, m]
            copies = [
                go(passed.at[low], got.at[low], sem + 4, dev(axis, c3)),
                go(passed.at[high], got.at[high], sem + 5, dev(axis, c1)),
            ]
            for m in range(m_count):
                keep[m] = u[c, m] + r[0, m]
            yield
            for copy in copies:
                copy.wait_recv()
            for m in range(m_count):
                put(m, keep[m] + got[m])

    running, finished = {}, set()

    def go_on(*which):
        for f in which:
            if f not in running:
                g = FLOWS[f][0]
                if g in crossing:
                    crossing.pop(g).wait_recv()
                running[f] = flow(f)
            if next(running[f], True):
                finished.add(f)

    def gather(g, everyone=False):
        first, n = GROUPS[g]
        q, at = n // 8 * T, first // 8 * T
        assert all(f in finished for f in range(len(FLOWS)) if FLOWS[f][0] == g)

        def copy_of(d, source):
            to = (sec + d) % 8 if everyone else (sec + 2 * d) % 8
            return remote(
                own.at[:, pl.ds(at, q)], full.at[:, ds(place_of(source), q)],
                s4.at[g, d - 1], q4.at[g, d - 1], (to, me),
            )

        def place_of(source):
            return first * T + source % 2 * (n // 2 * T) + source // 2 * q

        gathering[g] = []
        for d in range(1, 8) if everyone else (1, 2, 3):
            copy = copy_of(d, sec)
            copy.start()
            sends.append(copy)
            gathering[g].append(copy_of(d, (sec + 8 - (d if everyone else 2 * d)) % 8))
        full[:, ds(place_of(sec), q)] = own[:, at : at + q]

    def share(g):
        first, n = GROUPS[g]
        w = n // 2 * T
        for copy in gathering[g]:
            copy.wait_recv()

        def copy_of(c):
            where = full.at[:, ds(first * T + c * w, w)]
            return remote(where, where, s4.at[g, 7], q4.at[g, 7], other_core)

        copy = copy_of(core)
        copy.start()
        sends.append(copy)
        gathering[g] = [copy_of(1 - core)]

    l_vol.wait()
    l_cot.wait()
    pl.semaphore_wait(barrier, len(peers))
    pushed = {}
    for n, d in enumerate((3, -3, 2, -2, 1, -1)):
        pushed[-d] = push(n, vol, h_vol.at[3 - d], around[d])
    cot_pair = swap(6, cot.at[pl.ds(0, 64)], cot.at[pl.ds(64, 64)], h_cot)
    r, c = iotas((64, T))
    twice = one_hot(r == (c & 63))
    l_wf.wait()
    zero = jnp.zeros((64, T), BF)
    for ox in range(3):
        wx[ox * 640 : ox * 640 + 576, :] = wf[ox * 576 : (ox + 1) * 576, :]
        wx[ox * 640 + 576 : (ox + 1) * 640, :] = zero
    own_layers = layers_of(mm(vol[...], twice).astype(BF))
    spread_narrow(b_v, own_layers, 6 * 64)
    spread(b_d, own_layers, 64)
    for d in (-1, 1, -2, 2, -3, 3):
        pushed[d].wait_recv()
        got = inside(mm(h_vol[3 + d], twice), 2 * (me + d), 32, 64)
        spread_narrow(b_v, layers_of(got), (3 + d) * T)
    z1_all = conv(b_v, wx, 768, 64)
    z1[...] = z1_all[320:448]
    h1[...] = inside(silu(z1_all), 2 * me - 5, 32, 64)
    spread(b_1, layers_of(h1))
    l_we.wait()
    z2_all = conv(b_1, we, 640, 64)
    z2[...] = z2_all[256:384]
    sk[...] = inside(silu(z2_all), 2 * me - 4, 32, 64)
    for n in range(5):
        moved = mm(perm[...], sk[n * T : (n + 1) * T]).astype(BF)
        for t in range(8):
            blocks[n * 16 : (n + 1) * 16, t * T : (t + 1) * T] = moved[t * 16 : (t + 1) * 16]
    l_wd.wait()
    z3 = mm(blocks[...], wd[...])
    g1 = silu(z3).astype(BF)
    spread_coarse(b_c, [g1[n * 16 : (n + 1) * 16] for n in range(5)])
    l_wb.wait()
    z4 = conv(b_c, wb, 48, 16)
    g2 = inside(silu(z4), me - 1, 16, 16)
    l_wu.wait()
    lifted = mm(g2, wu[...]).astype(BF)
    for n in range(3):
        li[n * T : (n + 1) * T] = mm(perm_t[...], stacked(lifted[n * 16 : (n + 1) * 16])).astype(BF)
    layers = [
        jnp.concatenate([li[n * 64 : (n + 1) * 64], sk[(n + 2) * 64 : (n + 3) * 64]], axis=1) for n in range(6)
    ]
    spread(b_j, layers, 0, 1, 256)
    l_wj.wait()
    z7 = conv(b_j, wj, 256, 64)
    dec_o[...] = silu(z7[64:192]).astype(BF)

    lo, hi = arrived(cot_pair, h_cot)
    cots = jnp.concatenate([lo, cot[...], hi], axis=0)
    t7[...] = (cots.astype(F32) * slope(z7)).astype(BF)
    spread(b_s, layers_of(t7))
    back = conv_back(b_s, wj, T, 64)
    e_skip[...] = back[:, T:256]
    moved = mm(perm[...], back[:, 0:T].astype(BF)).astype(BF)
    lift_blocks = jnp.concatenate([moved[t * 16 : (t + 1) * 16] for t in range(8)], axis=1)
    e3 = mm_t(lift_blocks, wu[...]).astype(BF)
    t4[...] = (e3.astype(F32) * slope(z4[16:32])).astype(BF)
    pair = swap(8, t4, t4, h_t4)
    for t in range(8):
        diag[t * 16 : (t + 1) * 16, t * 256 : (t + 1) * 256] = g2[16:32]
    moved_t = turned(moved)
    for t in range(8):
        up = mm(moved_t, diag[:, t * 256 : (t + 1) * 256]).astype(BF)
        for b in range(8):
            at = UP_AT * T + (b % 4) * 256
            packed[2 * t + b // 4, :, at : at + 256] = up[b * 16 : (b + 1) * 16]
    step_t = turned(t4[...])
    grad_256(step_t, window(b_c, 16, 16, 16, 2), 0, 8, BOTTOM_AT)
    cross(0)
    grad_256(step_t, window(b_c, 16, 16, 16, 2), 8, 24, BOTTOM_AT)
    cross(1)
    grad_256(step_t, window(b_c, 16, 16, 16, 2), 24, 40, BOTTOM_AT)
    cross(2)
    grad_256(step_t, window(b_c, 16, 16, 16, 2), 40, 54, BOTTOM_AT)
    step_t = turned(t7[64:192])
    grad_128(step_t, window(b_j, 64, 64, T, 3), 54, 27, 3, JOIN_AT, 0, 3)
    cross(3)
    grad_128(step_t, window(b_j, 64, 64, T, 3), 54, 27, 3, JOIN_AT, 3, 27)
    cross(4)
    go_on(0)
    lo, hi = arrived(pair, h_t4)
    spread_coarse(b_4, [lo, t4[...], hi])
    e4 = conv_back(b_4, wb, 16, 16).astype(BF)
    t3 = (e4.astype(F32) * slope(z3[32:48])).astype(BF)
    e5 = stacked(mm_t(t3, wd[...]))
    high = e5.astype(BF)
    low = (e5 - high.astype(F32)).astype(BF)
    e5 = mm(perm_t[...], high) + mm(perm_t[...], low)
    t2[...] = ((e5 + e_skip[...]) * slope(z2[...])).astype(BF)
    pair = swap(10, t2.at[pl.ds(0, 64)], t2.at[pl.ds(64, 64)], h_t2)
    go_on(1, 3, 2, 4)
    grad_256(turned(t3), lambda n: blocks[32:48, n * T : (n + 2) * T], 0, 8, DOWN_AT)
    grad_128(turned(t2[...]), window(b_1, 256, 64, T, 1), 27, 14, 1, ENC_AT)
    cross(5)
    go_on(5, 6, 0)
    spread(b_s, layers_of(t2), 64)
    before_own = inside(mm(h_vol[2], twice), 2 * (me - 1), 32, 64)
    after_own = inside(mm(h_vol[4], twice), 2 * (me + 1), 32, 64)
    spread(b_d, [before_own[64:128]], 0)
    spread(b_d, [after_own[0:64]], 192)
    lo, hi = arrived(pair, h_t2)
    spread(b_s, [lo], 0)
    spread(b_s, [hi], 192)
    back = conv_back(b_s, we, T, 64)
    t1 = (back.astype(BF).astype(F32) * slope(z1[...])).astype(BF)
    for j in range(14):
        left, right = (b_d[t // 9 * 64 : 128 + t // 9 * 64, t % 9 * T : (t % 9 + 1) * T] for t in (2 * j, min(2 * j + 1, 26)))
        tile = left * half_mask[0]
        if j < 13:
            tile = tile + right * half_mask[1]
        a_f[:, j * T : (j + 1) * T] = tile
    grad_128(turned(t1), lambda n: a_f[:, n * T : (n + 1) * T], 14, 7, 1, FIRST_AT)
    cross(6)
    go_on(1, 7, 3, 8, 2, 4, 9, 5, 0, 6, 1, 3, 7, 8, 2, 4, 9, 5, 0, 6, 1, 3, 7, 8, 2, 4, 9, 5, 0, 6, 1, 3, 2, 7, 4)
    gather(3)
    go_on(8)
    gather(2)
    go_on(9, 5, 0)
    gather(0)
    go_on(6)
    gather(4)
    go_on(1)
    gather(1)
    go_on(7, 8)
    gather(5, True)
    share(2)
    go_on(9)
    gather(6, True)
    share(3)
    share(0)
    share(1)
    share(4)
    for g in (0, 1, 2, 3, 4, 5, 6):
        first, n = GROUPS[g]
        for copy in gathering[g]:
            copy.wait_recv()
        full_o[:, first * T : (first + n) * T] = full[:, first * T : (first + n) * T]
    for copy in sends:
        copy.wait_send()


def finish(dec, full, dec_o, gf_o, ge_o, gd_o, gb_o, gu_o, gj_o):
    factor = 1.0 / math.sqrt(16384)
    dec_o[...] = dec[...]

    def rows(tile, width):
        return full[:, tile * T : tile * T + width].astype(F32) * factor

    both = rows(JOIN_AT, 3456)
    gj_o[:, 0:3456] = both[0:8]
    gj_o[:, 3456:6912] = both[8:16]
    for b in range(4):
        gu_o[b * 16 : (b + 1) * 16, :] = rows(UP_AT + 2 * b, 256)
    gb_o[...] = rows(BOTTOM_AT, 6912)
    gd_o[...] = rows(DOWN_AT, 1024)
    both = rows(ENC_AT, 1792)
    ge_o[:, 0:1792] = both[0:8]
    ge_o[:, 1792:3456] = both[8:16, 0:1664]
    both = rows(FIRST_AT, 896)
    gf_o[:, 0:896] = both[0:8]
    gf_o[:, 896:1728] = both[8:16, 0:832]


def flow_scratch(tiles, how):
    v, w = lambda *shape: pltpu.VMEM((*shape, 16, tiles * T), BF), (16, 4, 1)
    two = [how[i] == "b" for i in range(3)]
    return {
        "u": [v(4, m) for m in w],
        "r": [v(2 if two[i] else 3, m) for i, m in enumerate(w)],
        **{name: [v(m) if two[i] else v(1) for i, m in enumerate(w)] for name in ("keep", "pass", "got")},
        "send": pltpu.SemaphoreType.DMA((18,)),
        "recv": pltpu.SemaphoreType.DMA((18,)),
    }


def scratch():
    v, dma = pltpu.VMEM, pltpu.SemaphoreType.DMA
    return [
        v((128, 64), BF), v((1728, 128), BF), v((3456, 128), BF), v((1024, 256), BF), v((6912, 256), BF),
        v((256, 1024), BF), v((6912, 128), BF), v((128, 128), BF), dma((8,)),
        v((9, 64, 64), BF), v((144, 16), BF), v((T, T), BF), v((T, T), BF), v((256, 256), BF), v((2, T, T), BF),
        v((5, 64, T), BF), v((256, 1152), BF), v((1920, T), BF), v((896, 640), BF), v((768, 1152), BF), v((384, 2304), BF), v((256, 1152), BF),
        v((80, 2304), BF), v((48, 2304), BF), v((T, 1792), BF), v((80, 1024), BF), v((T, 2048), BF),
        v((T, T), F32), v((T, T), F32), v((T, T), F32),
        v((768, T), BF), v((640, T), BF), v((384, T), BF), v((256, T), BF), v((T, T), BF), v((16, 256), BF),
        v((7, T, 64), BF), v((2, 64, T), BF), v((2, 64, T), BF), v((2, 16, 256), BF), dma((12,)), dma((12,)),
        v((16, 16, COLS), BF), v((16, 16, HALF), BF), v((16, EIGHTH), BF), v((16, COLS), BF),
        dma((8,)), dma((8,)), dma((8, 8)), dma((8, 8)), [flow_scratch(*f[3:]) for f in FLOWS],
    ]


def body(volume, w_first, w_enc, w_down, w_bottom, w_up, w_join, cotangent):
    out = lambda shape, dtype=F32: jax.ShapeDtypeStruct(shape, dtype)
    done = pl.pallas_call(
        kernel,
        out_shape=(out((128, 128), BF), out((16, COLS), BF)),
        in_specs=[pl.BlockSpec(memory_space=pl.ANY)] * 8,
        out_specs=[pl.BlockSpec(memory_space=pltpu.VMEM)] * 2,
        scratch_shapes=scratch(),
        compiler_params=pltpu.CompilerParams(
            collective_id=0, has_side_effects=True, vmem_limit_bytes=58 * 1024 * 1024
        ),
        name="step",
    )(
        volume.reshape(128, 64), w_first, w_enc, w_down, w_bottom, w_up, w_join, cotangent.reshape(128, 128)
    )
    results = pl.pallas_call(
        finish,
        out_shape=(
            out((128, 128), BF), out((8, 1728)), out((8, 3456)), out((16, 1024)), out((16, 6912)), out((64, 256)),
            out((8, 6912)),
        ),
        name="finish",
    )(*done)
    decoded, *grads = results
    return (decoded.reshape(1, 2, 8, 8, 128), *(g.T for g in grads))


def solution(mesh):
    crops = P("section", "space", None, None, None)
    return jax.shard_map(
        body,
        mesh=mesh,
        in_specs=(crops, P(), P(), P(), P(), P(), P(), crops),
        out_specs=(crops, *([P(None, "space")] * 6)),
        check_vma=False,
    )
```
